128 devices in a mesh: gz: 8 (over x, z_hi), tile: 16 (over z_lo, y, core).
Axes of the slice: x: 4, y: 4, z: 4 (z_hi: 2, z_lo: 2; z = z_hi * 2 + z_lo), core: 2. Of those that a mesh axis runs over, the one named last changes fastest.
Arguments:
- disp: float32 [16, 2, 128, 5120], P('gz', None, 'tile'), may hold values from -6 to 6
- vel: float32 [16, 2, 128, 5120], P('gz', None, 'tile'), may hold values from -4 to 4
- stiff_class: int32 [16, 128, 5120], P('gz', 'tile'), may hold values from 0 to 7
- valid: int32 [16, 128, 5120], P('gz', 'tile'), may hold values 0 or 1
- class_table: float32 [8], replicated, may hold values from 0.3 to 3
- warp: float32 [16, 3, 2], P('gz'), may hold values from 0 to 1
- spring_z: float32 [16, 3], P('gz'), may hold values from 1.2 to 2
- skip_partner: int32 [16], replicated, may hold values from 0 to 15, as said below
Outputs:
- disp_out: float32 [16, 2, 128, 5120], P('gz', None, 'tile')
- vel_out: float32 [16, 2, 128, 5120], P('gz', None, 'tile')
The draws below stay inside these ranges and needn't reach their ends.
Inputs may be any that keep to these rules, and one draw needn't show every extreme that they name: `skip_partner`: each section's partner lies in another z-block of 2 consecutive sections; the sections of one z-block have at most 1 partners inside any one other z-block, and exactly 1 inside some.
All inputs are finite; a program needn't handle non-finite values. No bound on the sum of `valid` on one device may be relied on, other than what follows from the above.
Results may differ from the reference program's by a relative error of at most 0.0003.
Values sent between devices are 32-bit elements; how exact they have to be, the bound alone decides.
A program may use at most 128 MiB of HBM per device.

```python
import math
import jax
import jax.numpy as jnp
from jax import lax

SEC_DEV = 2
COLS = 5120
ITERS = 3
NCLASS = 8
SECTIONS = 16
NR = 128


def shuffled(key):
    return jax.random.permutation(key, SEC_DEV)


def draw_skip_partner(key, part):
    blocks = SECTIONS // SEC_DEV
    bound = SEC_DEV // 2
    key_base, key_order, key_within = jax.random.split(key, 3)
    base = jax.random.randint(key_base, (blocks,), 0, blocks - 1)
    order = jax.vmap(shuffled)(jax.random.split(key_order, blocks))
    offset = 1 + (base[:, None] + order // bound) % (blocks - 1)
    target = (jnp.arange(blocks)[:, None] + offset) % blocks
    within = jax.random.randint(key_within, (blocks, SEC_DEV), 0, SEC_DEV)
    return (target * SEC_DEV + within).reshape(-1).astype(jnp.int32)


def section_signs(key):
    picks = jax.random.randint(jax.random.fold_in(key, 11), (SECTIONS,), 0, 2)
    return (2 * picks - 1).astype(jnp.float32)[:, None, None, None]


def draw_disp(key, part):
    signs = section_signs(key)
    key_amp, key_noise = jax.random.split(jax.random.fold_in(key, 21))
    amp = jax.random.uniform(key_amp, (SECTIONS, 2, 1, 1), jnp.float32, 3.5, 4.5)
    noise = jnp.clip(0.8 * jax.random.normal(key_noise, (SECTIONS, 2, NR, COLS), jnp.float32), -1.5, 1.5)
    return (signs * amp + noise).astype(jnp.float32)


def draw_vel(key, part):
    signs = section_signs(key)
    key_amp, key_noise = jax.random.split(jax.random.fold_in(key, 31))
    amp = jax.random.uniform(key_amp, (SECTIONS, 2, 1, 1), jnp.float32, 1.5, 2.5)
    noise = jnp.clip(0.5 * jax.random.normal(key_noise, (SECTIONS, 2, NR, COLS), jnp.float32), -1.2, 1.2)
    return (noise - signs * amp).astype(jnp.float32)


def place_ends(entries, own_key, least, high):
    spot = [jax.random.randint(jax.random.fold_in(own_key, axis), (), 0, length) for axis, length in enumerate(entries.shape)]
    widest = entries.shape.index(max(entries.shape))
    neighbour = spot[:widest] + [(spot[widest] + 1) % entries.shape[widest]] + spot[widest + 1:]
    return entries.at[tuple(spot)].set(least).at[tuple(neighbour)].set(high)


def level_of(rng, dims, cuts, least, top_value):
    factor_of, own = 1.0, jax.random.fold_in(rng, 6)
    for position, shards_of in cuts:
        draws = jnp.exp(jax.random.uniform(jax.random.fold_in(own, position), (shards_of,), jnp.float32, least / len(cuts), top_value / len(cuts)))
        factor_of = factor_of * jnp.repeat(draws, dims[position] // shards_of).reshape([-1 if axis == position else 1 for axis in range(len(dims))])
    return factor_of


def setup_inputs(seed: int = 0) -> dict:
    key_list = jax.random.split(jax.random.key(seed), 9)
    disp = draw_disp(jax.random.fold_in(key_list[8], 71), 0)
    vel = draw_vel(jax.random.fold_in(key_list[8], 71), 0)
    stiff_class = place_ends(jax.random.randint(key_list[2], (SECTIONS, NR, COLS), 0, NCLASS), jax.random.fold_in(key_list[2], 1), 0, NCLASS - 1).astype(jnp.int32)
    valid = place_ends((jax.random.randint(key_list[3], (SECTIONS, NR, COLS), 0, 8) < 7).astype(jnp.int32), jax.random.fold_in(key_list[3], 1), 0, 1)
    class_table = jnp.clip(jnp.exp(jax.random.uniform(key_list[4], (NCLASS,), jnp.float32, math.log(0.3), math.log(3.0))), 0.3, 3.0)
    warp = jnp.clip(1.0 * jax.random.uniform(key_list[5], (SECTIONS, 3, 2), jnp.float32) ** level_of(key_list[5], (SECTIONS, 3, 2), ((0, 8),), -0.2, 0.2), 0.0, 1.0)
    spring_z = jnp.clip(jnp.exp(math.log(2.0) - 0.5108256 * jax.random.uniform(key_list[6], (SECTIONS, 3), jnp.float32) ** level_of(key_list[6], (SECTIONS, 3), ((0, 8),), -0.2, 0.2)), 1.2, 2.0)
    skip_partner = draw_skip_partner(jax.random.fold_in(key_list[8], 71), 0)
    return dict(disp=disp, vel=vel, stiff_class=stiff_class, valid=valid, class_table=class_table, warp=warp, spring_z=spring_z, skip_partner=skip_partner)


DAMPING = 0.9
STEP = 0.1


def shift_left(field):
    return jnp.concatenate([field[..., 1:], jnp.zeros_like(field[..., :1])], axis=-1)


def shift_right(field):
    return jnp.concatenate([jnp.zeros_like(field[..., :1]), field[..., :-1]], axis=-1)


def warped(source, frac_row, frac_col):
    frac_row = frac_row[:, None, None, None]
    frac_col = frac_col[:, None, None, None]
    upper = source[:, :, 1:-1]
    lower = source[:, :, 2:]
    return ((1.0 - frac_row) * (1.0 - frac_col) * upper + (1.0 - frac_row) * frac_col * shift_left(upper)
            + frac_row * (1.0 - frac_col) * lower + frac_row * frac_col * shift_left(lower))


def section_force(field_ext, stiff_ext, prev_ext, next_ext, partner_ext, warp, spring_z, has_prev, has_next):
    center = field_ext[:, :, 1:-1]
    stiff_mid = stiff_ext[:, None, 1:-1]
    stiff_up = stiff_ext[:, None, :-2]
    stiff_down = stiff_ext[:, None, 2:]
    inplane = stiff_mid * (stiff_up * (field_ext[:, :, :-2] - center) + stiff_down * (field_ext[:, :, 2:] - center)
                           + shift_right(stiff_mid) * (shift_right(center) - center)
                           + shift_left(stiff_mid) * (shift_left(center) - center))
    pull = spring_z[:, 0][:, None, None, None] * has_prev[:, None, None, None] * (warped(prev_ext, warp[:, 0, 0], warp[:, 0, 1]) - center)
    pull = pull + spring_z[:, 1][:, None, None, None] * has_next[:, None, None, None] * (warped(next_ext, warp[:, 1, 0], warp[:, 1, 1]) - center)
    pull = pull + spring_z[:, 2][:, None, None, None] * (warped(partner_ext, warp[:, 2, 0], warp[:, 2, 1]) - center)
    return inplane + pull


def reference(disp, vel, stiff_class, valid, class_table, warp, spring_z, skip_partner):
    alive = valid.astype(jnp.float32)
    kappa = jnp.take(class_table, stiff_class) * alive
    stiff_ext = jnp.pad(kappa, ((0, 0), (1, 1), (0, 0)))
    section_ids = jnp.arange(SECTIONS, dtype=jnp.int32)
    field = disp
    velocity = vel
    for step in range(ITERS):
        field_ext = jnp.pad(field, ((0, 0), (0, 0), (1, 1), (0, 0)))

        def one_section(index):
            prev_id = jnp.maximum(index - 1, 0).astype(jnp.int32)
            next_id = jnp.minimum(index + 1, SECTIONS - 1).astype(jnp.int32)
            partner_id = lax.dynamic_slice_in_dim(skip_partner, index, 1, 0)[0].astype(jnp.int32)
            has_prev = jnp.reshape((index > 0).astype(jnp.float32), (1,))
            has_next = jnp.reshape((index < SECTIONS - 1).astype(jnp.float32), (1,))
            return section_force(
                lax.dynamic_slice_in_dim(field_ext, index, 1, 0),
                lax.dynamic_slice_in_dim(stiff_ext, index, 1, 0),
                lax.dynamic_slice_in_dim(field_ext, prev_id, 1, 0),
                lax.dynamic_slice_in_dim(field_ext, next_id, 1, 0),
                lax.dynamic_slice_in_dim(field_ext, partner_id, 1, 0),
                lax.dynamic_slice_in_dim(warp, index, 1, 0),
                lax.dynamic_slice_in_dim(spring_z, index, 1, 0),
                has_prev, has_next)[0]

        force = lax.map(one_section, section_ids)
        velocity = alive[:, None] * (DAMPING * velocity + STEP * force)
        field = field + STEP * velocity
    return field, velocity
```

```python
import jax
import jax.numpy as jnp
from jax import lax
from jax.sharding import PartitionSpec as P

ITERS = 3


DAMPING = 0.9
STEP = 0.1


def shift_rows(block, axis, forward):
    count = lax.axis_size(axis)
    pairs = [(i, i + 1) for i in range(count - 1)]
    if not forward:
        pairs = [(t, s) for s, t in pairs]
    return lax.ppermute(block, axis, pairs)


def shift_left(field):
    return jnp.concatenate([field[..., 1:], jnp.zeros_like(field[..., :1])], axis=-1)


def shift_right(field):
    return jnp.concatenate([jnp.zeros_like(field[..., :1]), field[..., :-1]], axis=-1)


def warped9(source, frac_row, frac_col):
    upper = source[:, :-1]
    lower = source[:, 1:]
    return (
        (1.0 - frac_row) * (1.0 - frac_col) * upper
        + (1.0 - frac_row) * frac_col * shift_left(upper)
        + frac_row * (1.0 - frac_col) * lower
        + frac_row * frac_col * shift_left(lower)
    )


def body(disp, vel, stiff_class, valid, class_table, warp, spring_z, skip_partner):
    local_count = disp.shape[0]
    block_count = lax.axis_size("gz")
    block_index = lax.axis_index("gz")
    total = local_count * block_count
    alive = valid.astype(jnp.float32)
    kappa = jnp.zeros(stiff_class.shape, jnp.float32)
    for level in range(class_table.shape[0]):
        kappa = jnp.where(stiff_class == level, class_table[level], kappa)
    kappa = kappa * alive
    stiff = jnp.stack([kappa, alive])
    stiff_ext = jnp.concatenate(
        [
            shift_rows(stiff[:, :, -1:], "tile", True),
            stiff,
            shift_rows(stiff[:, :, :1], "tile", False),
        ],
        axis=2,
    )
    kap_ext = stiff_ext[0]
    alive_mid = alive
    global_ids = block_index * local_count + jnp.arange(local_count, dtype=jnp.int32)
    has_prev = (global_ids > 0).astype(jnp.float32)
    has_next = (global_ids < total - 1).astype(jnp.float32)

    mine = lax.dynamic_slice_in_dim(skip_partner, block_index * local_count, local_count, 0)
    src_block = mine // local_count
    wanted = skip_partner.reshape(block_count, local_count)
    hit = (wanted // local_count) == block_index
    send_sel = jnp.sum(jnp.where(hit, wanted % local_count, 0), axis=1)

    field = disp
    velocity = vel
    for step in range(ITERS):
        send = field[0][None]
        for l in range(1, local_count):
            send = jnp.where((send_sel == l)[:, None, None, None], field[l][None], send)
        recv = lax.all_to_all(send, "gz", 0, 0, tiled=True)
        partner8 = jnp.stack(
            [lax.dynamic_index_in_dim(recv, src_block[l], 0, keepdims=False) for l in range(local_count)]
        )
        prev_face = shift_rows(field[-1], "gz", True)
        next_face = shift_rows(field[0], "gz", False)
        up = shift_rows(field[:, :, -1:], "tile", True)
        down = shift_rows(field[:, :, :1], "tile", False)
        field_ext = jnp.concatenate([up, field, down], axis=2)
        firsts = jnp.concatenate(
            [prev_face[None, :, :1], next_face[None, :, :1], partner8[:, :, :1]], axis=0
        )
        below = shift_rows(firsts, "tile", False)
        prev9 = [jnp.concatenate([prev_face, below[0]], axis=1)] + [
            field_ext[l - 1, :, 1:] for l in range(1, local_count)
        ]
        next9 = [field_ext[l + 1, :, 1:] for l in range(local_count - 1)] + [
            jnp.concatenate([next_face, below[1]], axis=1)
        ]
        forces = []
        for l in range(local_count):
            center = field[l]
            k_mid = kap_ext[l, 1:-1][None]
            k_up = kap_ext[l, :-2][None]
            k_down = kap_ext[l, 2:][None]
            inplane = k_mid * (
                k_up * (field_ext[l, :, :-2] - center)
                + k_down * (field_ext[l, :, 2:] - center)
                + shift_right(k_mid) * (shift_right(center) - center)
                + shift_left(k_mid) * (shift_left(center) - center)
            )
            partner9 = jnp.concatenate([partner8[l], below[2 + l]], axis=1)
            pull = spring_z[l, 0] * has_prev[l] * (warped9(prev9[l], warp[l, 0, 0], warp[l, 0, 1]) - center)
            pull = pull + spring_z[l, 1] * has_next[l] * (
                warped9(next9[l], warp[l, 1, 0], warp[l, 1, 1]) - center
            )
            pull = pull + spring_z[l, 2] * (warped9(partner9, warp[l, 2, 0], warp[l, 2, 1]) - center)
            forces.append(inplane + pull)
        force = jnp.stack(forces)
        velocity = alive_mid[:, None] * (DAMPING * velocity + STEP * force)
        field = field + STEP * velocity
    return (field, velocity)


def solution(mesh):
    placed = (
        P("gz", None, "tile", None),
        P("gz", None, "tile", None),
        P("gz", "tile", None),
        P("gz", "tile", None),
        P(),
        P("gz", None, None),
        P("gz", None),
        P(),
    )
    return jax.shard_map(
        body,
        mesh=mesh,
        in_specs=placed,
        out_specs=(P("gz", None, "tile", None), P("gz", None, "tile", None)),
        check_vma=False,
    )
```

```python
import functools

import jax
import jax.numpy as jnp
from jax import lax
from jax.experimental import pallas as pl
from jax.experimental.pallas import tpu as pltpu
from jax.sharding import PartitionSpec as P

MESH = pl.DeviceIdType.MESH

ITERS = 3


DAMPING = 0.9
STEP = 0.1


def shift_rows(block, axis, forward):
    count = lax.axis_size(axis)
    pairs = [(i, i + 1) for i in range(count - 1)]
    if not forward:
        pairs = [(t, s) for s, t in pairs]
    return lax.ppermute(block, axis, pairs)


def shift_left(field):
    return jnp.concatenate([field[..., 1:], jnp.zeros_like(field[..., :1])], axis=-1)


def shift_right(field):
    return jnp.concatenate([jnp.zeros_like(field[..., :1]), field[..., :-1]], axis=-1)


def warped9(source, frac_row, frac_col):
    upper = source[:, :-1]
    lower = source[:, 1:]
    return (
        (1.0 - frac_row) * (1.0 - frac_col) * upper
        + (1.0 - frac_row) * frac_col * shift_left(upper)
        + frac_row * (1.0 - frac_col) * lower
        + frac_row * frac_col * shift_left(lower)
    )


def gz_kernel(nb, send_ref, own_ref, recv_ref, prev_ref, next_ref, send_sems, recv_sems):
    me = lax.axis_index("gz")
    last = own_ref.shape[0] - 1
    barrier = pltpu.get_barrier_semaphore()
    for k in range(1, nb):
        pl.semaphore_signal(
            barrier, inc=1, device_id={"gz": lax.rem(me + k, nb)}, device_id_type=MESH
        )
    pl.semaphore_wait(barrier, nb - 1)
    copies = []
    for k in range(1, nb):
        dest = lax.rem(me + k, nb)
        copies.append(
            pltpu.make_async_remote_copy(
                src_ref=send_ref.at[dest],
                dst_ref=recv_ref.at[me],
                send_sem=send_sems.at[k],
                recv_sem=recv_sems.at[k],
                device_id={"gz": dest},
                device_id_type=MESH,
            )
        )
    copies.append(
        pltpu.make_async_remote_copy(
            src_ref=own_ref.at[last],
            dst_ref=prev_ref,
            send_sem=send_sems.at[nb],
            recv_sem=recv_sems.at[nb],
            device_id={"gz": lax.rem(me + 1, nb)},
            device_id_type=MESH,
        )
    )
    copies.append(
        pltpu.make_async_remote_copy(
            src_ref=own_ref.at[0],
            dst_ref=next_ref,
            send_sem=send_sems.at[nb + 1],
            recv_sem=recv_sems.at[nb + 1],
            device_id={"gz": lax.rem(me + nb - 1, nb)},
            device_id_type=MESH,
        )
    )
    for c in copies:
        c.start()
    for c in copies:
        c.wait()


def gz_exchange(send, own):
    nb = send.shape[0]
    face = own.shape[1:]
    moved = 4 * (send.size + 2 * own[0].size)
    return pl.pallas_call(
        functools.partial(gz_kernel, nb),
        out_shape=(
            jax.ShapeDtypeStruct(send.shape, send.dtype),
            jax.ShapeDtypeStruct(face, own.dtype),
            jax.ShapeDtypeStruct(face, own.dtype),
        ),
        in_specs=[pl.BlockSpec(memory_space=pl.ANY)] * 2,
        out_specs=[pl.BlockSpec(memory_space=pl.ANY)] * 3,
        scratch_shapes=[pltpu.SemaphoreType.DMA((nb + 2,)), pltpu.SemaphoreType.DMA((nb + 2,))],
        compiler_params=pltpu.CompilerParams(collective_id=0, has_side_effects=True),
        cost_estimate=pl.CostEstimate(flops=0, bytes_accessed=2 * moved, transcendentals=0),
    )(send, own)


def body(disp, vel, stiff_class, valid, class_table, warp, spring_z, skip_partner):
    local_count = disp.shape[0]
    block_count = lax.axis_size("gz")
    block_index = lax.axis_index("gz")
    total = local_count * block_count
    alive = valid.astype(jnp.float32)
    kappa = jnp.zeros(stiff_class.shape, jnp.float32)
    for level in range(class_table.shape[0]):
        kappa = jnp.where(stiff_class == level, class_table[level], kappa)
    kappa = kappa * alive
    stiff = jnp.stack([kappa, alive])
    stiff_ext = jnp.concatenate(
        [
            shift_rows(stiff[:, :, -1:], "tile", True),
            stiff,
            shift_rows(stiff[:, :, :1], "tile", False),
        ],
        axis=2,
    )
    kap_ext = stiff_ext[0]
    alive_mid = alive
    global_ids = block_index * local_count + jnp.arange(local_count, dtype=jnp.int32)
    has_prev = (global_ids > 0).astype(jnp.float32)
    has_next = (global_ids < total - 1).astype(jnp.float32)

    mine = lax.dynamic_slice_in_dim(skip_partner, block_index * local_count, local_count, 0)
    src_block = mine // local_count
    wanted = skip_partner.reshape(block_count, local_count)
    hit = (wanted // local_count) == block_index
    send_sel = jnp.sum(jnp.where(hit, wanted % local_count, 0), axis=1)

    field = disp
    velocity = vel
    for step in range(ITERS):
        send = field[0][None]
        for l in range(1, local_count):
            send = jnp.where((send_sel == l)[:, None, None, None], field[l][None], send)
        recv, prev_face, next_face = gz_exchange(send, field)
        partner8 = jnp.stack(
            [lax.dynamic_index_in_dim(recv, src_block[l], 0, keepdims=False) for l in range(local_count)]
        )
        up = shift_rows(field[:, :, -1:], "tile", True)
        down = shift_rows(field[:, :, :1], "tile", False)
        field_ext = jnp.concatenate([up, field, down], axis=2)
        firsts = jnp.concatenate(
            [prev_face[None, :, :1], next_face[None, :, :1], partner8[:, :, :1]], axis=0
        )
        below = shift_rows(firsts, "tile", False)
        prev9 = [jnp.concatenate([prev_face, below[0]], axis=1)] + [
            field_ext[l - 1, :, 1:] for l in range(1, local_count)
        ]
        next9 = [field_ext[l + 1, :, 1:] for l in range(local_count - 1)] + [
            jnp.concatenate([next_face, below[1]], axis=1)
        ]
        forces = []
        for l in range(local_count):
            center = field[l]
            k_mid = kap_ext[l, 1:-1][None]
            k_up = kap_ext[l, :-2][None]
            k_down = kap_ext[l, 2:][None]
            inplane = k_mid * (
                k_up * (field_ext[l, :, :-2] - center)
                + k_down * (field_ext[l, :, 2:] - center)
                + shift_right(k_mid) * (shift_right(center) - center)
                + shift_left(k_mid) * (shift_left(center) - center)
            )
            partner9 = jnp.concatenate([partner8[l], below[2 + l]], axis=1)
            pull = spring_z[l, 0] * has_prev[l] * (warped9(prev9[l], warp[l, 0, 0], warp[l, 0, 1]) - center)
            pull = pull + spring_z[l, 1] * has_next[l] * (
                warped9(next9[l], warp[l, 1, 0], warp[l, 1, 1]) - center
            )
            pull = pull + spring_z[l, 2] * (warped9(partner9, warp[l, 2, 0], warp[l, 2, 1]) - center)
            forces.append(inplane + pull)
        force = jnp.stack(forces)
        velocity = alive_mid[:, None] * (DAMPING * velocity + STEP * force)
        field = field + STEP * velocity
    return (field, velocity)


def solution(mesh):
    placed = (
        P("gz", None, "tile", None),
        P("gz", None, "tile", None),
        P("gz", "tile", None),
        P("gz", "tile", None),
        P(),
        P("gz", None, None),
        P("gz", None),
        P(),
    )
    return jax.shard_map(
        body,
        mesh=mesh,
        in_specs=placed,
        out_specs=(P("gz", None, "tile", None), P("gz", None, "tile", None)),
        check_vma=False,
    )
```

```python
import jax
import jax.numpy as jnp
from jax import lax
from jax.experimental import pallas as pl
from jax.experimental.pallas import tpu as pltpu
from jax.sharding import PartitionSpec as P


ITERS = 3


DAMPING = 0.9
STEP = 0.1


def shift_rows(block, axis, forward):
    count = lax.axis_size(axis)
    pairs = [(i, i + 1) for i in range(count - 1)]
    if not forward:
        pairs = [(t, s) for s, t in pairs]
    return lax.ppermute(block, axis, pairs)


def shift_left(field):
    return jnp.concatenate([field[..., 1:], jnp.zeros_like(field[..., :1])], axis=-1)


def shift_right(field):
    return jnp.concatenate([jnp.zeros_like(field[..., :1]), field[..., :-1]], axis=-1)


def update_kernel(scal_ref, sel_ref, x_ref, v_ref, k_ref, alive_ref, part_ref, up_ref, down_ref,
                  prevf_ref, nextf_ref, below_ref, xo_ref, vo_ref, send_ref):
    L, ncomp, R, C = x_ref.shape
    rows = lax.broadcasted_iota(jnp.int32, (R, C), 0)
    cols = lax.broadcasted_iota(jnp.int32, (R, C), 1)
    first_row = rows == 0
    last_row = rows == R - 1

    def shl(a):
        return jnp.where(cols == C - 1, 0.0, pltpu.roll(a, C - 1, 1))

    def shr(a):
        return jnp.where(cols == 0, 0.0, pltpu.roll(a, 1, 1))

    def warp_of(src, row8, w):
        lower = jnp.where(last_row, row8, pltpu.roll(src, R - 1, 0))
        return w[0] * src + w[1] * shl(src) + w[2] * lower + w[3] * shl(lower)

    for l in range(L):
        ws = []
        for k in range(3):
            a = scal_ref[l, 3 + 2 * k]
            b = scal_ref[l, 4 + 2 * k]
            ws.append(((1.0 - a) * (1.0 - b), (1.0 - a) * b, a * (1.0 - b), a * b))
        k_up = k_ref[0, l]
        k_mid = k_ref[1, l]
        k_dn = k_ref[2, l]
        k_r = k_ref[3, l]
        k_l = k_ref[4, l]
        alive = alive_ref[l]
        for c in range(ncomp):
            x = x_ref[l, c]
            x_up = jnp.where(first_row, up_ref[pl.ds(l * ncomp + c, 1), :], pltpu.roll(x, 1, 0))
            x_dn = jnp.where(last_row, down_ref[pl.ds(l * ncomp + c, 1), :], pltpu.roll(x, R - 1, 0))
            inplane = k_mid * (
                k_up * (x_up - x) + k_dn * (x_dn - x) + k_r * (shr(x) - x) + k_l * (shl(x) - x)
            )
            if l == 0:
                prev_src, prev_row = prevf_ref[c], below_ref[pl.ds(c, 1), :]
            else:
                prev_src, prev_row = x_ref[l - 1, c], down_ref[pl.ds((l - 1) * ncomp + c, 1), :]
            if l == L - 1:
                next_src, next_row = nextf_ref[c], below_ref[pl.ds(ncomp + c, 1), :]
            else:
                next_src, next_row = x_ref[l + 1, c], down_ref[pl.ds((l + 1) * ncomp + c, 1), :]
            part_row = below_ref[pl.ds((2 + l) * ncomp + c, 1), :]
            pull = scal_ref[l, 0] * (warp_of(prev_src, prev_row, ws[0]) - x)
            pull = pull + scal_ref[l, 1] * (warp_of(next_src, next_row, ws[1]) - x)
            pull = pull + scal_ref[l, 2] * (warp_of(part_ref[l, c], part_row, ws[2]) - x)
            force = inplane + pull
            vel = alive * (DAMPING * v_ref[l, c] + STEP * force)
            vo_ref[l, c] = vel
            xo_ref[l, c] = x + STEP * vel
    for d in range(send_ref.shape[0]):
        send_ref[d] = xo_ref[sel_ref[d]]


def update(scal, sel, x, v, kst, alive, part, up, down, prevf, nextf, below):
    nb = sel.shape[0]
    vmem = pl.BlockSpec(memory_space=pltpu.VMEM)
    smem = pl.BlockSpec(memory_space=pltpu.SMEM)
    moved = 4 * (3 * x.size + kst.size + alive.size + part.size + 3 * x[0].size + nb * x[0].size)
    return pl.pallas_call(
        update_kernel,
        out_shape=(
            jax.ShapeDtypeStruct(x.shape, x.dtype),
            jax.ShapeDtypeStruct(x.shape, x.dtype),
            jax.ShapeDtypeStruct((nb,) + x.shape[1:], x.dtype),
        ),
        in_specs=[smem, smem] + [vmem] * 10,
        out_specs=[vmem] * 3,
        compiler_params=pltpu.CompilerParams(vmem_limit_bytes=48 * 1024 * 1024),
        cost_estimate=pl.CostEstimate(flops=80 * x.size, bytes_accessed=moved, transcendentals=0),
    )(scal, sel, x, v, kst, alive, part, up, down, prevf, nextf, below)


def body(disp, vel, stiff_class, valid, class_table, warp, spring_z, skip_partner):
    local_count = disp.shape[0]
    block_count = lax.axis_size("gz")
    block_index = lax.axis_index("gz")
    total = local_count * block_count
    alive = valid.astype(jnp.float32)
    kappa = jnp.zeros(stiff_class.shape, jnp.float32)
    for level in range(class_table.shape[0]):
        kappa = jnp.where(stiff_class == level, class_table[level], kappa)
    kappa = kappa * alive
    stiff = jnp.stack([kappa, alive])
    stiff_ext = jnp.concatenate(
        [
            shift_rows(stiff[:, :, -1:], "tile", True),
            stiff,
            shift_rows(stiff[:, :, :1], "tile", False),
        ],
        axis=2,
    )
    kap_ext = stiff_ext[0]
    alive_mid = alive
    global_ids = block_index * local_count + jnp.arange(local_count, dtype=jnp.int32)
    has_prev = (global_ids > 0).astype(jnp.float32)
    has_next = (global_ids < total - 1).astype(jnp.float32)

    mine = lax.dynamic_slice_in_dim(skip_partner, block_index * local_count, local_count, 0)
    src_block = mine // local_count
    wanted = skip_partner.reshape(block_count, local_count)
    hit = (wanted // local_count) == block_index
    send_sel = jnp.sum(jnp.where(hit, wanted % local_count, 0), axis=1)

    k_mid = kap_ext[:, 1:-1]
    kst = jnp.stack([kap_ext[:, :-2], k_mid, kap_ext[:, 2:], shift_right(k_mid), shift_left(k_mid)])
    scal = jnp.concatenate(
        [
            (spring_z[:, 0] * has_prev)[:, None],
            (spring_z[:, 1] * has_next)[:, None],
            spring_z[:, 2:3],
            warp.reshape(local_count, 6),
        ],
        axis=1,
    )
    ncomp = disp.shape[1]
    cols = disp.shape[3]

    field = disp
    velocity = vel
    send = field[0][None]
    for l in range(1, local_count):
        send = jnp.where((send_sel == l)[:, None, None, None], field[l][None], send)
    for _ in range(ITERS):
      recv = lax.all_to_all(send, "gz", 0, 0, tiled=True)
      partner8 = jnp.stack(
          [lax.dynamic_index_in_dim(recv, src_block[l], 0, keepdims=False) for l in range(local_count)]
      )
      prev_face = shift_rows(field[-1], "gz", True)
      next_face = shift_rows(field[0], "gz", False)
      up = shift_rows(field[:, :, -1:], "tile", True)
      down = shift_rows(field[:, :, :1], "tile", False)
      firsts = jnp.concatenate(
          [prev_face[None, :, :1], next_face[None, :, :1], partner8[:, :, :1]], axis=0
      )
      below = shift_rows(firsts, "tile", False)
      field, velocity, send = update(
          scal,
          send_sel,
          field,
          velocity,
          kst,
          alive_mid,
          partner8,
          up.reshape(local_count * ncomp, cols),
          down.reshape(local_count * ncomp, cols),
          prev_face,
          next_face,
          below.reshape((2 + local_count) * ncomp, cols),
      )
    return (field, velocity)


def solution(mesh):
    placed = (
        P("gz", None, "tile", None),
        P("gz", None, "tile", None),
        P("gz", "tile", None),
        P("gz", "tile", None),
        P(),
        P("gz", None, None),
        P("gz", None),
        P(),
    )
    return jax.shard_map(
        body,
        mesh=mesh,
        in_specs=placed,
        out_specs=(P("gz", None, "tile", None), P("gz", None, "tile", None)),
        check_vma=False,
    )
```

```python
import jax
import jax.numpy as jnp
from jax import lax
from jax.experimental import pallas as pl
from jax.experimental.pallas import tpu as pltpu
from jax.sharding import PartitionSpec as P


ITERS = 3


DAMPING = 0.9
STEP = 0.1


def shift_rows(block, axis, forward):
    count = lax.axis_size(axis)
    pairs = [(i, i + 1) for i in range(count - 1)]
    if not forward:
        pairs = [(t, s) for s, t in pairs]
    return lax.ppermute(block, axis, pairs)


def shift_left(field):
    return jnp.concatenate([field[..., 1:], jnp.zeros_like(field[..., :1])], axis=-1)


def shift_right(field):
    return jnp.concatenate([jnp.zeros_like(field[..., :1]), field[..., :-1]], axis=-1)


def update_kernel(scal_ref, sel_ref, x_ref, v_ref, k_ref, alive_ref, part_ref, up_ref, down_ref,
                  prevf_ref, nextf_ref, below_ref, xo_ref, vo_ref, send_ref, lastf_ref, firstf_ref,
                  top_ref, bot_ref):
    L, ncomp, R, C = x_ref.shape
    rows = lax.broadcasted_iota(jnp.int32, (R, C), 0)
    cols = lax.broadcasted_iota(jnp.int32, (R, C), 1)
    first_row = rows == 0
    last_row = rows == R - 1

    def shl(a):
        return jnp.where(cols == C - 1, 0.0, pltpu.roll(a, C - 1, 1))

    def shr(a):
        return jnp.where(cols == 0, 0.0, pltpu.roll(a, 1, 1))

    def warp_of(src, row8, w):
        lower = jnp.where(last_row, row8, pltpu.roll(src, R - 1, 0))
        return w[0] * src + w[1] * shl(src) + w[2] * lower + w[3] * shl(lower)

    for l in range(L):
        ws = []
        for k in range(3):
            a = scal_ref[l, 3 + 2 * k]
            b = scal_ref[l, 4 + 2 * k]
            ws.append(((1.0 - a) * (1.0 - b), (1.0 - a) * b, a * (1.0 - b), a * b))
        k_up = k_ref[0, l]
        k_mid = k_ref[1, l]
        k_dn = k_ref[2, l]
        k_r = k_ref[3, l]
        k_l = k_ref[4, l]
        alive = alive_ref[l]
        for c in range(ncomp):
            x = x_ref[l, c]
            x_up = jnp.where(first_row, up_ref[pl.ds(l * ncomp + c, 1), :], pltpu.roll(x, 1, 0))
            x_dn = jnp.where(last_row, down_ref[pl.ds(l * ncomp + c, 1), :], pltpu.roll(x, R - 1, 0))
            inplane = k_mid * (
                k_up * (x_up - x) + k_dn * (x_dn - x) + k_r * (shr(x) - x) + k_l * (shl(x) - x)
            )
            if l == 0:
                prev_src, prev_row = prevf_ref[c], below_ref[pl.ds(c, 1), :]
            else:
                prev_src, prev_row = x_ref[l - 1, c], down_ref[pl.ds((l - 1) * ncomp + c, 1), :]
            if l == L - 1:
                next_src, next_row = nextf_ref[c], below_ref[pl.ds(ncomp + c, 1), :]
            else:
                next_src, next_row = x_ref[l + 1, c], down_ref[pl.ds((l + 1) * ncomp + c, 1), :]
            part_row = below_ref[pl.ds((2 + l) * ncomp + c, 1), :]
            pull = scal_ref[l, 0] * (warp_of(prev_src, prev_row, ws[0]) - x)
            pull = pull + scal_ref[l, 1] * (warp_of(next_src, next_row, ws[1]) - x)
            pull = pull + scal_ref[l, 2] * (warp_of(part_ref[l, c], part_row, ws[2]) - x)
            force = inplane + pull
            vel = alive * (DAMPING * v_ref[l, c] + STEP * force)
            vo_ref[l, c] = vel
            new = x + STEP * vel
            xo_ref[l, c] = new
            if l == L - 1:
                lastf_ref[c] = new
            if l == 0:
                firstf_ref[c] = new
            top_ref[pl.ds(l * ncomp + c, 1), :] = new[0:1]
            bot_ref[pl.ds(l * ncomp + c, 1), :] = new[R - 1 : R]
    for d in range(send_ref.shape[0]):
        send_ref[d] = xo_ref[sel_ref[d]]


def update(scal, sel, x, v, kst, alive, part, up, down, prevf, nextf, below):
    nb = sel.shape[0]
    vmem = pl.BlockSpec(memory_space=pltpu.VMEM)
    smem = pl.BlockSpec(memory_space=pltpu.SMEM)
    moved = 4 * (3 * x.size + kst.size + alive.size + part.size + 3 * x[0].size + nb * x[0].size)
    return pl.pallas_call(
        update_kernel,
        out_shape=(
            jax.ShapeDtypeStruct(x.shape, x.dtype),
            jax.ShapeDtypeStruct(x.shape, x.dtype),
            jax.ShapeDtypeStruct((nb,) + x.shape[1:], x.dtype),
            jax.ShapeDtypeStruct(x.shape[1:], x.dtype),
            jax.ShapeDtypeStruct(x.shape[1:], x.dtype),
            jax.ShapeDtypeStruct((x.shape[0] * x.shape[1], x.shape[3]), x.dtype),
            jax.ShapeDtypeStruct((x.shape[0] * x.shape[1], x.shape[3]), x.dtype),
        ),
        in_specs=[smem, smem] + [vmem] * 10,
        out_specs=[vmem] * 7,
        compiler_params=pltpu.CompilerParams(vmem_limit_bytes=48 * 1024 * 1024),
        cost_estimate=pl.CostEstimate(flops=80 * x.size, bytes_accessed=moved, transcendentals=0),
    )(scal, sel, x, v, kst, alive, part, up, down, prevf, nextf, below)


def body(disp, vel, stiff_class, valid, class_table, warp, spring_z, skip_partner):
    local_count = disp.shape[0]
    block_count = lax.axis_size("gz")
    block_index = lax.axis_index("gz")
    total = local_count * block_count
    alive = valid.astype(jnp.float32)
    kappa = jnp.zeros(stiff_class.shape, jnp.float32)
    for level in range(class_table.shape[0]):
        kappa = jnp.where(stiff_class == level, class_table[level], kappa)
    kappa = kappa * alive
    stiff = jnp.stack([kappa, alive])
    stiff_ext = jnp.concatenate(
        [
            shift_rows(stiff[:, :, -1:], "tile", True),
            stiff,
            shift_rows(stiff[:, :, :1], "tile", False),
        ],
        axis=2,
    )
    kap_ext = stiff_ext[0]
    alive_mid = alive
    global_ids = block_index * local_count + jnp.arange(local_count, dtype=jnp.int32)
    has_prev = (global_ids > 0).astype(jnp.float32)
    has_next = (global_ids < total - 1).astype(jnp.float32)

    mine = lax.dynamic_slice_in_dim(skip_partner, block_index * local_count, local_count, 0)
    src_block = mine // local_count
    wanted = skip_partner.reshape(block_count, local_count)
    hit = (wanted // local_count) == block_index
    send_sel = jnp.sum(jnp.where(hit, wanted % local_count, 0), axis=1)

    k_mid = kap_ext[:, 1:-1]
    kst = jnp.stack([kap_ext[:, :-2], k_mid, kap_ext[:, 2:], shift_right(k_mid), shift_left(k_mid)])
    scal = jnp.concatenate(
        [
            (spring_z[:, 0] * has_prev)[:, None],
            (spring_z[:, 1] * has_next)[:, None],
            spring_z[:, 2:3],
            warp.reshape(local_count, 6),
        ],
        axis=1,
    )
    ncomp = disp.shape[1]
    cols = disp.shape[3]

    field = disp
    velocity = vel
    send = field[0][None]
    for l in range(1, local_count):
        send = jnp.where((send_sel == l)[:, None, None, None], field[l][None], send)
    last_face = field[-1]
    first_face = field[0]
    top_rows = field[:, :, 0].reshape(local_count * ncomp, cols)
    bot_rows = field[:, :, -1].reshape(local_count * ncomp, cols)
    for _ in range(ITERS):
      recv = lax.all_to_all(send, "gz", 0, 0, tiled=True)
      partner8 = jnp.stack(
          [lax.dynamic_index_in_dim(recv, src_block[l], 0, keepdims=False) for l in range(local_count)]
      )
      prev_face = shift_rows(last_face, "gz", True)
      next_face = shift_rows(first_face, "gz", False)
      up = shift_rows(bot_rows, "tile", True)
      down = shift_rows(top_rows, "tile", False)
      firsts = jnp.concatenate(
          [prev_face[:, 0], next_face[:, 0]] + [partner8[l, :, 0] for l in range(local_count)], axis=0
      )
      below = shift_rows(firsts, "tile", False)
      field, velocity, send, last_face, first_face, top_rows, bot_rows = update(
          scal,
          send_sel,
          field,
          velocity,
          kst,
          alive_mid,
          partner8,
          up,
          down,
          prev_face,
          next_face,
          below,
      )
    return (field, velocity)


def solution(mesh):
    placed = (
        P("gz", None, "tile", None),
        P("gz", None, "tile", None),
        P("gz", "tile", None),
        P("gz", "tile", None),
        P(),
        P("gz", None, None),
        P("gz", None),
        P(),
    )
    return jax.shard_map(
        body,
        mesh=mesh,
        in_specs=placed,
        out_specs=(P("gz", None, "tile", None), P("gz", None, "tile", None)),
        check_vma=False,
    )
```

```python
import jax
import jax.numpy as jnp
from jax import lax
from jax.experimental import pallas as pl
from jax.experimental.pallas import tpu as pltpu
from jax.sharding import PartitionSpec as P


ITERS = 3


DAMPING = 0.9
STEP = 0.1


def shift_rows(block, axis, forward):
    count = lax.axis_size(axis)
    pairs = [(i, i + 1) for i in range(count - 1)]
    if not forward:
        pairs = [(t, s) for s, t in pairs]
    return lax.ppermute(block, axis, pairs)


def shift_left(field):
    return jnp.concatenate([field[..., 1:], jnp.zeros_like(field[..., :1])], axis=-1)


def shift_right(field):
    return jnp.concatenate([jnp.zeros_like(field[..., :1]), field[..., :-1]], axis=-1)


def update_kernel(scal_ref, sel_ref, x_ref, v_ref, k_ref, alive_ref, part_ref, up_ref, down_ref,
                  prevf_ref, nextf_ref, below_ref, xo_ref, vo_ref, send_ref, lastf_ref, firstf_ref,
                  top_ref, bot_ref):
    L, ncomp, R, C = x_ref.shape
    rows = lax.broadcasted_iota(jnp.int32, (R, C), 0)
    cols = lax.broadcasted_iota(jnp.int32, (R, C), 1)
    first_row = rows == 0
    last_row = rows == R - 1

    def shl(a):
        return jnp.where(cols == C - 1, 0.0, pltpu.roll(a, C - 1, 1))

    def shr(a):
        return jnp.where(cols == 0, 0.0, pltpu.roll(a, 1, 1))

    def warp_of(src, row8, w):
        lower = jnp.where(last_row, row8, pltpu.roll(src, R - 1, 0))
        return w[0] * src + w[1] * shl(src) + w[2] * lower + w[3] * shl(lower)

    for l in range(L):
        ws = []
        for k in range(3):
            a = scal_ref[l, 3 + 2 * k]
            b = scal_ref[l, 4 + 2 * k]
            ws.append(((1.0 - a) * (1.0 - b), (1.0 - a) * b, a * (1.0 - b), a * b))
        k_up = k_ref[0, l]
        k_mid = k_ref[1, l]
        k_dn = k_ref[2, l]
        k_r = k_ref[3, l]
        k_l = k_ref[4, l]
        alive = alive_ref[l]
        for c in range(ncomp):
            x = x_ref[l, c]
            x_up = jnp.where(first_row, up_ref[pl.ds(l * ncomp + c, 1), :], pltpu.roll(x, 1, 0))
            x_dn = jnp.where(last_row, down_ref[pl.ds(l * ncomp + c, 1), :], pltpu.roll(x, R - 1, 0))
            inplane = k_mid * (
                k_up * (x_up - x) + k_dn * (x_dn - x) + k_r * (shr(x) - x) + k_l * (shl(x) - x)
            )
            if l == 0:
                prev_src, prev_row = prevf_ref[pl.ds(c * R, R), :], below_ref[pl.ds(c, 1), :]
            else:
                prev_src, prev_row = x_ref[l - 1, c], down_ref[pl.ds((l - 1) * ncomp + c, 1), :]
            if l == L - 1:
                next_src, next_row = nextf_ref[pl.ds(c * R, R), :], below_ref[pl.ds(ncomp + c, 1), :]
            else:
                next_src, next_row = x_ref[l + 1, c], down_ref[pl.ds((l + 1) * ncomp + c, 1), :]
            part_row = below_ref[pl.ds((2 + l) * ncomp + c, 1), :]
            pull = scal_ref[l, 0] * (warp_of(prev_src, prev_row, ws[0]) - x)
            pull = pull + scal_ref[l, 1] * (warp_of(next_src, next_row, ws[1]) - x)
            pull = pull + scal_ref[l, 2] * (warp_of(part_ref[l, pl.ds(c * R, R), :], part_row, ws[2]) - x)
            force = inplane + pull
            vel = alive * (DAMPING * v_ref[l, c] + STEP * force)
            vo_ref[l, c] = vel
            new = x + STEP * vel
            xo_ref[l, c] = new
            if l == L - 1:
                lastf_ref[pl.ds(c * R, R), :] = new
            if l == 0:
                firstf_ref[pl.ds(c * R, R), :] = new
            top_ref[pl.ds(l * ncomp + c, 1), :] = new[0:1]
            bot_ref[pl.ds(l * ncomp + c, 1), :] = new[R - 1 : R]
    for d in range(send_ref.shape[0]):
        for c in range(ncomp):
            send_ref[d, pl.ds(c * R, R), :] = xo_ref[sel_ref[d], c]


def update(scal, sel, x, v, kst, alive, part, up, down, prevf, nextf, below):
    nb = sel.shape[0]
    vmem = pl.BlockSpec(memory_space=pltpu.VMEM)
    smem = pl.BlockSpec(memory_space=pltpu.SMEM)
    moved = 4 * (3 * x.size + kst.size + alive.size + part.size + 3 * x[0].size + nb * x[0].size)
    return pl.pallas_call(
        update_kernel,
        out_shape=(
            jax.ShapeDtypeStruct(x.shape, x.dtype),
            jax.ShapeDtypeStruct(x.shape, x.dtype),
            jax.ShapeDtypeStruct((nb, x.shape[1] * x.shape[2], x.shape[3]), x.dtype),
            jax.ShapeDtypeStruct((x.shape[1] * x.shape[2], x.shape[3]), x.dtype),
            jax.ShapeDtypeStruct((x.shape[1] * x.shape[2], x.shape[3]), x.dtype),
            jax.ShapeDtypeStruct((x.shape[0] * x.shape[1], x.shape[3]), x.dtype),
            jax.ShapeDtypeStruct((x.shape[0] * x.shape[1], x.shape[3]), x.dtype),
        ),
        in_specs=[smem, smem] + [vmem] * 10,
        out_specs=[vmem] * 7,
        compiler_params=pltpu.CompilerParams(vmem_limit_bytes=48 * 1024 * 1024),
        cost_estimate=pl.CostEstimate(flops=80 * x.size, bytes_accessed=moved, transcendentals=0),
    )(scal, sel, x, v, kst, alive, part, up, down, prevf, nextf, below)


def body(disp, vel, stiff_class, valid, class_table, warp, spring_z, skip_partner):
    local_count = disp.shape[0]
    block_count = lax.axis_size("gz")
    block_index = lax.axis_index("gz")
    total = local_count * block_count
    alive = valid.astype(jnp.float32)
    kappa = jnp.zeros(stiff_class.shape, jnp.float32)
    for level in range(class_table.shape[0]):
        kappa = jnp.where(stiff_class == level, class_table[level], kappa)
    kappa = kappa * alive
    stiff = jnp.stack([kappa, alive])
    stiff_ext = jnp.concatenate(
        [
            shift_rows(stiff[:, :, -1:], "tile", True),
            stiff,
            shift_rows(stiff[:, :, :1], "tile", False),
        ],
        axis=2,
    )
    kap_ext = stiff_ext[0]
    alive_mid = alive
    global_ids = block_index * local_count + jnp.arange(local_count, dtype=jnp.int32)
    has_prev = (global_ids > 0).astype(jnp.float32)
    has_next = (global_ids < total - 1).astype(jnp.float32)

    mine = lax.dynamic_slice_in_dim(skip_partner, block_index * local_count, local_count, 0)
    src_block = mine // local_count
    wanted = skip_partner.reshape(block_count, local_count)
    hit = (wanted // local_count) == block_index
    send_sel = jnp.sum(jnp.where(hit, wanted % local_count, 0), axis=1)

    k_mid = kap_ext[:, 1:-1]
    kst = jnp.stack([kap_ext[:, :-2], k_mid, kap_ext[:, 2:], shift_right(k_mid), shift_left(k_mid)])
    scal = jnp.concatenate(
        [
            (spring_z[:, 0] * has_prev)[:, None],
            (spring_z[:, 1] * has_next)[:, None],
            spring_z[:, 2:3],
            warp.reshape(local_count, 6),
        ],
        axis=1,
    )
    ncomp = disp.shape[1]
    cols = disp.shape[3]
    rows = disp.shape[2]

    states = []
    for c in range(ncomp):
        field = disp[:, c : c + 1]
        send = field[0][None]
        for l in range(1, local_count):
            send = jnp.where((send_sel == l)[:, None, None, None], field[l][None], send)
        states.append(
            dict(
                field=field,
                velocity=vel[:, c : c + 1],
                send=send.reshape(block_count, rows, cols),
                last_face=field[-1].reshape(rows, cols),
                first_face=field[0].reshape(rows, cols),
                top_rows=field[:, :, 0].reshape(local_count, cols),
                bot_rows=field[:, :, -1].reshape(local_count, cols),
            )
        )
    for _ in range(ITERS):
      for c in range(ncomp):
        st = states[c]
        recv = lax.all_to_all(st["send"], "gz", 0, 0, tiled=True)
        partner8 = jnp.stack(
            [lax.dynamic_index_in_dim(recv, src_block[l], 0, keepdims=False) for l in range(local_count)]
        )
        prev_face = shift_rows(st["last_face"], "gz", True)
        next_face = shift_rows(st["first_face"], "gz", False)
        up = shift_rows(st["bot_rows"], "tile", True)
        down = shift_rows(st["top_rows"], "tile", False)
        firsts = jnp.concatenate(
            [prev_face[::rows], next_face[::rows]] + [partner8[l, ::rows] for l in range(local_count)],
            axis=0,
        )
        below = shift_rows(firsts, "tile", False)
        outs = update(
            scal,
            send_sel,
            st["field"],
            st["velocity"],
            kst,
            alive_mid,
            partner8,
            up,
            down,
            prev_face,
            next_face,
            below,
        )
        keys = ("field", "velocity", "send", "last_face", "first_face", "top_rows", "bot_rows")
        states[c] = dict(zip(keys, outs))
    field = jnp.concatenate([st["field"] for st in states], axis=1)
    velocity = jnp.concatenate([st["velocity"] for st in states], axis=1)
    return (field, velocity)


def solution(mesh):
    placed = (
        P("gz", None, "tile", None),
        P("gz", None, "tile", None),
        P("gz", "tile", None),
        P("gz", "tile", None),
        P(),
        P("gz", None, None),
        P("gz", None),
        P(),
    )
    return jax.shard_map(
        body,
        mesh=mesh,
        in_specs=placed,
        out_specs=(P("gz", None, "tile", None), P("gz", None, "tile", None)),
        check_vma=False,
    )
```

```python
import jax
import jax.numpy as jnp
from jax import lax
from jax.experimental import pallas as pl
from jax.experimental.pallas import tpu as pltpu
from jax.sharding import PartitionSpec as P


ITERS = 3


DAMPING = 0.9
STEP = 0.1


def shift_rows(block, axis, forward):
    count = lax.axis_size(axis)
    pairs = [(i, i + 1) for i in range(count - 1)]
    if not forward:
        pairs = [(t, s) for s, t in pairs]
    return lax.ppermute(block, axis, pairs)


def shift_left(field):
    return jnp.concatenate([field[..., 1:], jnp.zeros_like(field[..., :1])], axis=-1)


def shift_right(field):
    return jnp.concatenate([jnp.zeros_like(field[..., :1]), field[..., :-1]], axis=-1)


def update_kernel(scal_ref, sel_ref, src_ref, x_ref, v_ref, k_ref, alive_ref, part_ref, up_ref, down_ref,
                  prevf_ref, nextf_ref, below_ref, xo_ref, vo_ref, send_ref, lastf_ref, firstf_ref,
                  top_ref, bot_ref):
    L, ncomp, R, C = x_ref.shape
    rows = lax.broadcasted_iota(jnp.int32, (R, C), 0)
    cols = lax.broadcasted_iota(jnp.int32, (R, C), 1)
    first_row = rows == 0
    last_row = rows == R - 1

    def shl(a):
        return jnp.where(cols == C - 1, 0.0, pltpu.roll(a, C - 1, 1))

    def shr(a):
        return jnp.where(cols == 0, 0.0, pltpu.roll(a, 1, 1))

    def warp_of(src, row8, w):
        lower = jnp.where(last_row, row8, pltpu.roll(src, R - 1, 0))
        return w[0] * src + w[1] * shl(src) + w[2] * lower + w[3] * shl(lower)

    for l in range(L):
        ws = []
        for k in range(3):
            a = scal_ref[l, 3 + 2 * k]
            b = scal_ref[l, 4 + 2 * k]
            ws.append(((1.0 - a) * (1.0 - b), (1.0 - a) * b, a * (1.0 - b), a * b))
        k_up = k_ref[0, l]
        k_mid = k_ref[1, l]
        k_dn = k_ref[2, l]
        k_r = k_ref[3, l]
        k_l = k_ref[4, l]
        alive = alive_ref[l]
        for c in range(ncomp):
            x = x_ref[l, c]
            x_up = jnp.where(first_row, up_ref[pl.ds(l * ncomp + c, 1), :], pltpu.roll(x, 1, 0))
            x_dn = jnp.where(last_row, down_ref[pl.ds(l * ncomp + c, 1), :], pltpu.roll(x, R - 1, 0))
            inplane = k_mid * (
                k_up * (x_up - x) + k_dn * (x_dn - x) + k_r * (shr(x) - x) + k_l * (shl(x) - x)
            )
            if l == 0:
                prev_src, prev_row = prevf_ref[pl.ds(c * R, R), :], below_ref[pl.ds(c, 1), :]
            else:
                prev_src, prev_row = x_ref[l - 1, c], down_ref[pl.ds((l - 1) * ncomp + c, 1), :]
            if l == L - 1:
                next_src, next_row = nextf_ref[pl.ds(c * R, R), :], below_ref[pl.ds(ncomp + c, 1), :]
            else:
                next_src, next_row = x_ref[l + 1, c], down_ref[pl.ds((l + 1) * ncomp + c, 1), :]
            part_row = below_ref[pl.ds((2 + l) * ncomp + c, 1), :]
            pull = scal_ref[l, 0] * (warp_of(prev_src, prev_row, ws[0]) - x)
            pull = pull + scal_ref[l, 1] * (warp_of(next_src, next_row, ws[1]) - x)
            pull = pull + scal_ref[l, 2] * (
                warp_of(part_ref[src_ref[l], pl.ds(c * R, R), :], part_row, ws[2]) - x
            )
            force = inplane + pull
            vel = alive * (DAMPING * v_ref[l, c] + STEP * force)
            vo_ref[l, c] = vel
            new = x + STEP * vel
            xo_ref[l, c] = new
            if l == L - 1:
                lastf_ref[pl.ds(c * R, R), :] = new
            if l == 0:
                firstf_ref[pl.ds(c * R, R), :] = new
            top_ref[pl.ds(l * ncomp + c, 1), :] = new[0:1]
            bot_ref[pl.ds(l * ncomp + c, 1), :] = new[R - 1 : R]
    for d in range(send_ref.shape[0]):
        for c in range(ncomp):
            send_ref[d, pl.ds(c * R, R), :] = xo_ref[sel_ref[d], c]


def update(scal, sel, src, x, v, kst, alive, part, up, down, prevf, nextf, below):
    nb = sel.shape[0]
    vmem = pl.BlockSpec(memory_space=pltpu.VMEM)
    smem = pl.BlockSpec(memory_space=pltpu.SMEM)
    moved = 4 * (3 * x.size + kst.size + alive.size + part.size + 3 * x[0].size + nb * x[0].size)
    return pl.pallas_call(
        update_kernel,
        out_shape=(
            jax.ShapeDtypeStruct(x.shape, x.dtype),
            jax.ShapeDtypeStruct(x.shape, x.dtype),
            jax.ShapeDtypeStruct((nb, x.shape[1] * x.shape[2], x.shape[3]), x.dtype),
            jax.ShapeDtypeStruct((x.shape[1] * x.shape[2], x.shape[3]), x.dtype),
            jax.ShapeDtypeStruct((x.shape[1] * x.shape[2], x.shape[3]), x.dtype),
            jax.ShapeDtypeStruct((x.shape[0] * x.shape[1], x.shape[3]), x.dtype),
            jax.ShapeDtypeStruct((x.shape[0] * x.shape[1], x.shape[3]), x.dtype),
        ),
        in_specs=[smem, smem, smem] + [vmem] * 10,
        out_specs=[vmem] * 7,
        compiler_params=pltpu.CompilerParams(vmem_limit_bytes=48 * 1024 * 1024),
        cost_estimate=pl.CostEstimate(flops=80 * x.size, bytes_accessed=moved, transcendentals=0),
    )(scal, sel, src, x, v, kst, alive, part, up, down, prevf, nextf, below)


def body(disp, vel, stiff_class, valid, class_table, warp, spring_z, skip_partner):
    local_count = disp.shape[0]
    block_count = lax.axis_size("gz")
    block_index = lax.axis_index("gz")
    total = local_count * block_count
    alive = valid.astype(jnp.float32)
    kappa = jnp.zeros(stiff_class.shape, jnp.float32)
    for level in range(class_table.shape[0]):
        kappa = jnp.where(stiff_class == level, class_table[level], kappa)
    kappa = kappa * alive
    stiff = jnp.stack([kappa, alive])
    stiff_ext = jnp.concatenate(
        [
            shift_rows(stiff[:, :, -1:], "tile", True),
            stiff,
            shift_rows(stiff[:, :, :1], "tile", False),
        ],
        axis=2,
    )
    kap_ext = stiff_ext[0]
    alive_mid = alive
    global_ids = block_index * local_count + jnp.arange(local_count, dtype=jnp.int32)
    has_prev = (global_ids > 0).astype(jnp.float32)
    has_next = (global_ids < total - 1).astype(jnp.float32)

    mine = lax.dynamic_slice_in_dim(skip_partner, block_index * local_count, local_count, 0)
    src_block = mine // local_count
    wanted = skip_partner.reshape(block_count, local_count)
    hit = (wanted // local_count) == block_index
    send_sel = jnp.sum(jnp.where(hit, wanted % local_count, 0), axis=1)
    send_sel = jnp.clip(send_sel, 0, local_count - 1)
    src_block = jnp.clip(src_block, 0, block_count - 1)

    k_mid = kap_ext[:, 1:-1]
    kst = jnp.stack([kap_ext[:, :-2], k_mid, kap_ext[:, 2:], shift_right(k_mid), shift_left(k_mid)])
    scal = jnp.concatenate(
        [
            (spring_z[:, 0] * has_prev)[:, None],
            (spring_z[:, 1] * has_next)[:, None],
            spring_z[:, 2:3],
            warp.reshape(local_count, 6),
        ],
        axis=1,
    )
    ncomp = disp.shape[1]
    cols = disp.shape[3]

    field = disp
    velocity = vel
    send = field[0][None]
    for l in range(1, local_count):
        send = jnp.where((send_sel == l)[:, None, None, None], field[l][None], send)
    plane = ncomp * disp.shape[2]
    send = send.reshape(block_count, plane, cols)
    last_face = field[-1].reshape(plane, cols)
    first_face = field[0].reshape(plane, cols)
    top_rows = field[:, :, 0].reshape(local_count * ncomp, cols)
    bot_rows = field[:, :, -1].reshape(local_count * ncomp, cols)
    for _ in range(ITERS):
      recv = lax.all_to_all(send, "gz", 0, 0, tiled=True)
      heads = recv[:, :: disp.shape[2]]
      partner_heads = jnp.stack(
          [lax.dynamic_index_in_dim(heads, src_block[l], 0, keepdims=False) for l in range(local_count)]
      )
      prev_face = shift_rows(last_face, "gz", True)
      next_face = shift_rows(first_face, "gz", False)
      up = shift_rows(bot_rows, "tile", True)
      down = shift_rows(top_rows, "tile", False)
      rows = disp.shape[2]
      firsts = jnp.concatenate(
          [prev_face[::rows], next_face[::rows]] + [partner_heads[l] for l in range(local_count)], axis=0
      )
      below = shift_rows(firsts, "tile", False)
      field, velocity, send, last_face, first_face, top_rows, bot_rows = update(
          scal,
          send_sel,
          src_block,
          field,
          velocity,
          kst,
          alive_mid,
          recv,
          up,
          down,
          prev_face,
          next_face,
          below,
      )
    return (field, velocity)


def solution(mesh):
    placed = (
        P("gz", None, "tile", None),
        P("gz", None, "tile", None),
        P("gz", "tile", None),
        P("gz", "tile", None),
        P(),
        P("gz", None, None),
        P("gz", None),
        P(),
    )
    return jax.shard_map(
        body,
        mesh=mesh,
        in_specs=placed,
        out_specs=(P("gz", None, "tile", None), P("gz", None, "tile", None)),
        check_vma=False,
    )
```

```python
import jax
import jax.numpy as jnp
from jax import lax
from jax.experimental import pallas as pl
from jax.experimental.pallas import tpu as pltpu
from jax.sharding import PartitionSpec as P


ITERS = 3


DAMPING = 0.9
STEP = 0.1


def shift_rows(block, axis, forward):
    count = lax.axis_size(axis)
    pairs = [(i, i + 1) for i in range(count - 1)]
    if not forward:
        pairs = [(t, s) for s, t in pairs]
    return lax.ppermute(block, axis, pairs)


def shift_left(field):
    return jnp.concatenate([field[..., 1:], jnp.zeros_like(field[..., :1])], axis=-1)


def shift_right(field):
    return jnp.concatenate([jnp.zeros_like(field[..., :1]), field[..., :-1]], axis=-1)


def update_kernel(scal_ref, sel_ref, x_ref, v_ref, k_ref, alive_ref, part_ref, up_ref, down_ref,
                  prevf_ref, nextf_ref, below_ref, xo_ref, vo_ref, send_ref, lastf_ref, firstf_ref,
                  top_ref, bot_ref):
    L, ncomp, R, C = x_ref.shape
    rows = lax.broadcasted_iota(jnp.int32, (R, C), 0)
    cols = lax.broadcasted_iota(jnp.int32, (R, C), 1)
    first_row = rows == 0
    last_row = rows == R - 1

    def shl(a):
        return jnp.where(cols == C - 1, 0.0, pltpu.roll(a, C - 1, 1))

    def shr(a):
        return jnp.where(cols == 0, 0.0, pltpu.roll(a, 1, 1))

    def warp_of(src, row8, w):
        lower = jnp.where(last_row, row8, pltpu.roll(src, R - 1, 0))
        return w[0] * src + w[1] * shl(src) + w[2] * lower + w[3] * shl(lower)

    for l in range(L):
        ws = []
        for k in range(3):
            a = scal_ref[l, 3 + 2 * k]
            b = scal_ref[l, 4 + 2 * k]
            ws.append(((1.0 - a) * (1.0 - b), (1.0 - a) * b, a * (1.0 - b), a * b))
        k_up = k_ref[0, l]
        k_mid = k_ref[1, l]
        k_dn = k_ref[2, l]
        k_r = k_ref[3, l]
        k_l = k_ref[4, l]
        alive = alive_ref[l]
        for c in range(ncomp):
            x = x_ref[l, c]
            x_up = jnp.where(first_row, up_ref[pl.ds(l * ncomp + c, 1), :], pltpu.roll(x, 1, 0))
            x_dn = jnp.where(last_row, down_ref[pl.ds(l * ncomp + c, 1), :], pltpu.roll(x, R - 1, 0))
            inplane = k_mid * (
                k_up * (x_up - x) + k_dn * (x_dn - x) + k_r * (shr(x) - x) + k_l * (shl(x) - x)
            )
            if l == 0:
                prev_src, prev_row = prevf_ref[pl.ds(c * R, R), :], below_ref[pl.ds(c, 1), :]
            else:
                prev_src, prev_row = x_ref[l - 1, c], down_ref[pl.ds((l - 1) * ncomp + c, 1), :]
            if l == L - 1:
                next_src, next_row = nextf_ref[pl.ds(c * R, R), :], below_ref[pl.ds(ncomp + c, 1), :]
            else:
                next_src, next_row = x_ref[l + 1, c], down_ref[pl.ds((l + 1) * ncomp + c, 1), :]
            part_row = below_ref[pl.ds((2 + l) * ncomp + c, 1), :]
            pull = scal_ref[l, 0] * (warp_of(prev_src, prev_row, ws[0]) - x)
            pull = pull + scal_ref[l, 1] * (warp_of(next_src, next_row, ws[1]) - x)
            pull = pull + scal_ref[l, 2] * (warp_of(part_ref[l, pl.ds(c * R, R), :], part_row, ws[2]) - x)
            force = inplane + pull
            vel = alive * (DAMPING * v_ref[l, c] + STEP * force)
            vo_ref[l, c] = vel
            new = x + STEP * vel
            xo_ref[l, c] = new
            if l == L - 1:
                lastf_ref[pl.ds(c * R, R), :] = new
            if l == 0:
                firstf_ref[pl.ds(c * R, R), :] = new
            top_ref[pl.ds(l * ncomp + c, 1), :] = new[0:1]
            bot_ref[pl.ds(l * ncomp + c, 1), :] = new[R - 1 : R]
    for d in range(send_ref.shape[0]):
        for c in range(ncomp):
            send_ref[d, pl.ds(c * R, R), :] = xo_ref[sel_ref[d], c]


def update(scal, sel, x, v, kst, alive, part, up, down, prevf, nextf, below):
    nb = sel.shape[0]
    vmem = pl.BlockSpec(memory_space=pltpu.VMEM)
    smem = pl.BlockSpec(memory_space=pltpu.SMEM)
    moved = 4 * (3 * x.size + kst.size + alive.size + part.size + 3 * x[0].size + nb * x[0].size)
    return pl.pallas_call(
        update_kernel,
        out_shape=(
            jax.ShapeDtypeStruct(x.shape, x.dtype),
            jax.ShapeDtypeStruct(x.shape, x.dtype),
            jax.ShapeDtypeStruct((nb, x.shape[1] * x.shape[2], x.shape[3]), x.dtype),
            jax.ShapeDtypeStruct((x.shape[1] * x.shape[2], x.shape[3]), x.dtype),
            jax.ShapeDtypeStruct((x.shape[1] * x.shape[2], x.shape[3]), x.dtype),
            jax.ShapeDtypeStruct((x.shape[0] * x.shape[1], x.shape[3]), x.dtype),
            jax.ShapeDtypeStruct((x.shape[0] * x.shape[1], x.shape[3]), x.dtype),
        ),
        in_specs=[smem, smem] + [vmem] * 10,
        out_specs=[vmem] * 7,
        compiler_params=pltpu.CompilerParams(vmem_limit_bytes=48 * 1024 * 1024),
        cost_estimate=pl.CostEstimate(flops=80 * x.size, bytes_accessed=moved, transcendentals=0),
    )(scal, sel, x, v, kst, alive, part, up, down, prevf, nextf, below)


def body(disp, vel, stiff_class, valid, class_table, warp, spring_z, skip_partner):
    local_count = disp.shape[0]
    block_count = lax.axis_size("gz")
    block_index = lax.axis_index("gz")
    total = local_count * block_count
    alive = valid.astype(jnp.float32)
    kappa = jnp.zeros(stiff_class.shape, jnp.float32)
    for level in range(class_table.shape[0]):
        kappa = jnp.where(stiff_class == level, class_table[level], kappa)
    kappa = kappa * alive
    stiff = jnp.stack([kappa, alive])
    stiff_ext = jnp.concatenate(
        [
            shift_rows(stiff[:, :, -1:], "tile", True),
            stiff,
            shift_rows(stiff[:, :, :1], "tile", False),
        ],
        axis=2,
    )
    kap_ext = stiff_ext[0]
    alive_mid = alive
    global_ids = block_index * local_count + jnp.arange(local_count, dtype=jnp.int32)
    has_prev = (global_ids > 0).astype(jnp.float32)
    has_next = (global_ids < total - 1).astype(jnp.float32)

    mine = lax.dynamic_slice_in_dim(skip_partner, block_index * local_count, local_count, 0)
    src_block = mine // local_count
    wanted = skip_partner.reshape(block_count, local_count)
    hit = (wanted // local_count) == block_index
    send_sel = jnp.sum(jnp.where(hit, wanted % local_count, 0), axis=1)

    k_mid = kap_ext[:, 1:-1]
    kst = jnp.stack([kap_ext[:, :-2], k_mid, kap_ext[:, 2:], shift_right(k_mid), shift_left(k_mid)])
    scal = jnp.concatenate(
        [
            (spring_z[:, 0] * has_prev)[:, None],
            (spring_z[:, 1] * has_next)[:, None],
            spring_z[:, 2:3],
            warp.reshape(local_count, 6),
        ],
        axis=1,
    )
    ncomp = disp.shape[1]
    cols = disp.shape[3]

    field = disp
    velocity = vel
    send = field[0][None]
    for l in range(1, local_count):
        send = jnp.where((send_sel == l)[:, None, None, None], field[l][None], send)
    plane = ncomp * disp.shape[2]
    send = send.reshape(block_count, plane, cols)
    last_face = field[-1].reshape(plane, cols)
    first_face = field[0].reshape(plane, cols)
    top_rows = field[:, :, 0].reshape(local_count * ncomp, cols)
    bot_rows = field[:, :, -1].reshape(local_count * ncomp, cols)
    for _ in range(ITERS):
      recv = lax.all_to_all(send, "gz", 0, 0, tiled=True)
      partner8 = jnp.stack(
          [lax.dynamic_index_in_dim(recv, src_block[l], 0, keepdims=False) for l in range(local_count)]
      )
      prev_face = shift_rows(last_face, "gz", True)
      next_face = shift_rows(first_face, "gz", False)
      up = shift_rows(bot_rows, "tile", True)
      down = shift_rows(top_rows, "tile", False)
      rows = disp.shape[2]
      heads = [prev_face, next_face] + [partner8[l] for l in range(local_count)]
      firsts = jnp.concatenate(
          [h[c * rows : c * rows + 1] for h in heads for c in range(ncomp)], axis=0
      )
      below = shift_rows(firsts, "tile", False)
      field, velocity, send, last_face, first_face, top_rows, bot_rows = update(
          scal,
          send_sel,
          field,
          velocity,
          kst,
          alive_mid,
          partner8,
          up,
          down,
          prev_face,
          next_face,
          below,
      )
    return (field, velocity)


def solution(mesh):
    placed = (
        P("gz", None, "tile", None),
        P("gz", None, "tile", None),
        P("gz", "tile", None),
        P("gz", "tile", None),
        P(),
        P("gz", None, None),
        P("gz", None),
        P(),
    )
    return jax.shard_map(
        body,
        mesh=mesh,
        in_specs=placed,
        out_specs=(P("gz", None, "tile", None), P("gz", None, "tile", None)),
        check_vma=False,
    )
```

```python
import jax
import jax.numpy as jnp
from jax import lax
from jax.experimental import pallas as pl
from jax.experimental.pallas import tpu as pltpu
from jax.sharding import PartitionSpec as P


ITERS = 3


DAMPING = 0.9
STEP = 0.1


def shift_rows(block, axis, forward):
    count = lax.axis_size(axis)
    pairs = [(i, i + 1) for i in range(count - 1)]
    if not forward:
        pairs = [(t, s) for s, t in pairs]
    return lax.ppermute(block, axis, pairs)


def shift_left(field):
    return jnp.concatenate([field[..., 1:], jnp.zeros_like(field[..., :1])], axis=-1)


def shift_right(field):
    return jnp.concatenate([jnp.zeros_like(field[..., :1]), field[..., :-1]], axis=-1)


def update_kernel(scal_ref, sel_ref, x_ref, v_ref, k_ref, alive_ref, part_ref, up_ref, down_ref,
                  prevf_ref, nextf_ref, below_ref, xo_ref, vo_ref, send_ref, lastf_ref, firstf_ref,
                  top_ref, bot_ref):
    L, ncomp, R, C = x_ref.shape
    rows = lax.broadcasted_iota(jnp.int32, (R, C), 0)
    cols = lax.broadcasted_iota(jnp.int32, (R, C), 1)
    first_row = rows == 0
    last_row = rows == R - 1

    def shl(a):
        return jnp.where(cols == C - 1, 0.0, pltpu.roll(a, C - 1, 1))

    def shr(a):
        return jnp.where(cols == 0, 0.0, pltpu.roll(a, 1, 1))

    def warp_of(src, row8, w):
        lower = jnp.where(last_row, row8, pltpu.roll(src, R - 1, 0))
        return w[0] * src + w[1] * shl(src) + w[2] * lower + w[3] * shl(lower)

    for l in range(L):
        ws = []
        for k in range(3):
            a = scal_ref[l, 3 + 2 * k]
            b = scal_ref[l, 4 + 2 * k]
            ws.append(((1.0 - a) * (1.0 - b), (1.0 - a) * b, a * (1.0 - b), a * b))
        k_up = k_ref[0, l]
        k_mid = k_ref[1, l]
        k_dn = k_ref[2, l]
        k_r = k_ref[3, l]
        k_l = k_ref[4, l]
        alive = alive_ref[l]
        for c in range(ncomp):
            x = x_ref[l, c]
            x_up = jnp.where(first_row, up_ref[pl.ds(l * ncomp + c, 1), :], pltpu.roll(x, 1, 0))
            x_dn = jnp.where(last_row, down_ref[pl.ds(l * ncomp + c, 1), :], pltpu.roll(x, R - 1, 0))
            inplane = k_mid * (
                k_up * (x_up - x) + k_dn * (x_dn - x) + k_r * (shr(x) - x) + k_l * (shl(x) - x)
            )
            if l == 0:
                prev_src, prev_row = prevf_ref[pl.ds(c * R, R), :], below_ref[pl.ds(c, 1), :]
            else:
                prev_src, prev_row = x_ref[l - 1, c], down_ref[pl.ds((l - 1) * ncomp + c, 1), :]
            if l == L - 1:
                next_src, next_row = nextf_ref[pl.ds(c * R, R), :], below_ref[pl.ds(ncomp + c, 1), :]
            else:
                next_src, next_row = x_ref[l + 1, c], down_ref[pl.ds((l + 1) * ncomp + c, 1), :]
            part_row = below_ref[pl.ds((2 + l) * ncomp + c, 1), :]
            pull = scal_ref[l, 0] * (warp_of(prev_src, prev_row, ws[0]) - x)
            pull = pull + scal_ref[l, 1] * (warp_of(next_src, next_row, ws[1]) - x)
            pull = pull + scal_ref[l, 2] * (warp_of(part_ref[l, pl.ds(c * R, R), :], part_row, ws[2]) - x)
            force = inplane + pull
            vel = alive * (DAMPING * v_ref[l, c] + STEP * force)
            vo_ref[l, c] = vel
            new = x + STEP * vel
            xo_ref[l, c] = new
            if l == L - 1:
                lastf_ref[pl.ds(c * R, R), :] = new
            if l == 0:
                firstf_ref[pl.ds(c * R, R), :] = new
            top_ref[pl.ds(l * ncomp + c, 1), :] = new[0:1]
            bot_ref[pl.ds(l * ncomp + c, 1), :] = new[R - 1 : R]
    for d in range(send_ref.shape[0]):
        for c in range(ncomp):
            send_ref[d, pl.ds(c * R, R), :] = xo_ref[sel_ref[d], c]


def update(scal, sel, x, v, kst, alive, part, up, down, prevf, nextf, below):
    nb = sel.shape[0]
    vmem = pl.BlockSpec(memory_space=pltpu.VMEM)
    smem = pl.BlockSpec(memory_space=pltpu.SMEM)
    moved = 4 * (3 * x.size + kst.size + alive.size + part.size + 3 * x[0].size + nb * x[0].size)
    return pl.pallas_call(
        update_kernel,
        out_shape=(
            jax.ShapeDtypeStruct(x.shape, x.dtype),
            jax.ShapeDtypeStruct(x.shape, x.dtype),
            jax.ShapeDtypeStruct((nb, x.shape[1] * x.shape[2], x.shape[3]), x.dtype),
            jax.ShapeDtypeStruct((x.shape[1] * x.shape[2], x.shape[3]), x.dtype),
            jax.ShapeDtypeStruct((x.shape[1] * x.shape[2], x.shape[3]), x.dtype),
            jax.ShapeDtypeStruct((x.shape[0] * x.shape[1], x.shape[3]), x.dtype),
            jax.ShapeDtypeStruct((x.shape[0] * x.shape[1], x.shape[3]), x.dtype),
        ),
        in_specs=[smem, smem] + [vmem] * 10,
        out_specs=[vmem] * 7,
        compiler_params=pltpu.CompilerParams(vmem_limit_bytes=48 * 1024 * 1024),
        cost_estimate=pl.CostEstimate(flops=80 * x.size, bytes_accessed=moved, transcendentals=0),
    )(scal, sel, x, v, kst, alive, part, up, down, prevf, nextf, below)


def body(disp, vel, stiff_class, valid, class_table, warp, spring_z, skip_partner):
    local_count = disp.shape[0]
    block_count = lax.axis_size("gz")
    block_index = lax.axis_index("gz")
    total = local_count * block_count
    alive = valid.astype(jnp.float32)
    kappa = jnp.zeros(stiff_class.shape, jnp.float32)
    for level in range(class_table.shape[0]):
        kappa = jnp.where(stiff_class == level, class_table[level], kappa)
    kappa = kappa * alive
    stiff = jnp.stack([kappa, alive])
    stiff_ext = jnp.concatenate(
        [
            shift_rows(stiff[:, :, -1:], "tile", True),
            stiff,
            shift_rows(stiff[:, :, :1], "tile", False),
        ],
        axis=2,
    )
    kap_ext = stiff_ext[0]
    alive_mid = alive
    global_ids = block_index * local_count + jnp.arange(local_count, dtype=jnp.int32)
    has_prev = (global_ids > 0).astype(jnp.float32)
    has_next = (global_ids < total - 1).astype(jnp.float32)

    mine = lax.dynamic_slice_in_dim(skip_partner, block_index * local_count, local_count, 0)
    src_block = mine // local_count
    wanted = skip_partner.reshape(block_count, local_count)
    hit = (wanted // local_count) == block_index
    send_sel = jnp.sum(jnp.where(hit, wanted % local_count, 0), axis=1)

    k_mid = kap_ext[:, 1:-1]
    kst = jnp.stack([kap_ext[:, :-2], k_mid, kap_ext[:, 2:], shift_right(k_mid), shift_left(k_mid)])
    scal = jnp.concatenate(
        [
            (spring_z[:, 0] * has_prev)[:, None],
            (spring_z[:, 1] * has_next)[:, None],
            spring_z[:, 2:3],
            warp.reshape(local_count, 6),
        ],
        axis=1,
    )
    ncomp = disp.shape[1]
    cols = disp.shape[3]

    field = disp
    velocity = vel
    send = field[0][None]
    for l in range(1, local_count):
        send = jnp.where((send_sel == l)[:, None, None, None], field[l][None], send)
    plane = ncomp * disp.shape[2]
    send = send.reshape(block_count, plane, cols)
    last_face = field[-1].reshape(plane, cols)
    first_face = field[0].reshape(plane, cols)
    top_rows = field[:, :, 0].reshape(local_count * ncomp, cols)
    bot_rows = field[:, :, -1].reshape(local_count * ncomp, cols)
    for _ in range(ITERS):
      recv = lax.all_to_all(send, "gz", 0, 0, tiled=True)
      partner8 = jnp.stack(
          [lax.dynamic_index_in_dim(recv, src_block[l], 0, keepdims=False) for l in range(local_count)]
      )
      prev_face = shift_rows(last_face, "gz", True)
      next_face = shift_rows(first_face, "gz", False)
      up = shift_rows(bot_rows, "tile", True)
      down = shift_rows(top_rows, "tile", False)
      rows = disp.shape[2]
      heads = [prev_face[c * rows : c * rows + 1] for c in range(ncomp)]
      heads += [next_face[c * rows : c * rows + 1] for c in range(ncomp)]
      heads += [
          lax.dynamic_slice(recv, (src_block[l], c * rows, 0), (1, 1, cols))[0]
          for l in range(local_count)
          for c in range(ncomp)
      ]
      firsts = jnp.concatenate(heads, axis=0)
      below = shift_rows(firsts, "tile", False)
      field, velocity, send, last_face, first_face, top_rows, bot_rows = update(
          scal,
          send_sel,
          field,
          velocity,
          kst,
          alive_mid,
          partner8,
          up,
          down,
          prev_face,
          next_face,
          below,
      )
    return (field, velocity)


def solution(mesh):
    placed = (
        P("gz", None, "tile", None),
        P("gz", None, "tile", None),
        P("gz", "tile", None),
        P("gz", "tile", None),
        P(),
        P("gz", None, None),
        P("gz", None),
        P(),
    )
    return jax.shard_map(
        body,
        mesh=mesh,
        in_specs=placed,
        out_specs=(P("gz", None, "tile", None), P("gz", None, "tile", None)),
        check_vma=False,
    )
```

```python
import jax
import jax.numpy as jnp
from jax import lax
from jax.experimental import pallas as pl
from jax.experimental.pallas import tpu as pltpu
from jax.sharding import PartitionSpec as P


ITERS = 3


DAMPING = 0.9
STEP = 0.1


def shift_rows(block, axis, forward):
    count = lax.axis_size(axis)
    pairs = [(i, i + 1) for i in range(count - 1)]
    if not forward:
        pairs = [(t, s) for s, t in pairs]
    return lax.ppermute(block, axis, pairs)


def shift_left(field):
    return jnp.concatenate([field[..., 1:], jnp.zeros_like(field[..., :1])], axis=-1)


def shift_right(field):
    return jnp.concatenate([jnp.zeros_like(field[..., :1]), field[..., :-1]], axis=-1)


def update_kernel(scal_ref, sel_ref, x_ref, v_ref, k_ref, alive_ref, part_ref, up_ref, down_ref,
                  prevf_ref, nextf_ref, below_ref, xo_ref, vo_ref, send_ref, lastf_ref, firstf_ref,
                  top_ref, bot_ref):
    L, ncomp, R, C = x_ref.shape
    rows = lax.broadcasted_iota(jnp.int32, (R, C), 0)
    cols = lax.broadcasted_iota(jnp.int32, (R, C), 1)
    first_row = rows == 0
    last_row = rows == R - 1

    def shl(a):
        return jnp.where(cols == C - 1, 0.0, pltpu.roll(a, C - 1, 1))

    def shr(a):
        return jnp.where(cols == 0, 0.0, pltpu.roll(a, 1, 1))

    def warp_of(src, row8, w):
        a, b = w
        across = (1.0 - b) * src + b * shl(src)
        across8 = (1.0 - b) * row8 + b * jnp.where(cols[0:1] == C - 1, 0.0, pltpu.roll(row8, C - 1, 1))
        lower = jnp.where(last_row, across8, pltpu.roll(across, R - 1, 0))
        return (1.0 - a) * across + a * lower

    for l in range(L):
        ws = []
        for k in range(3):
            a = scal_ref[l, 3 + 2 * k]
            b = scal_ref[l, 4 + 2 * k]
            ws.append((a, b))
        k_up = k_ref[0, l]
        k_mid = k_ref[1, l]
        k_dn = k_ref[2, l]
        k_r = k_ref[3, l]
        k_l = k_ref[4, l]
        alive = alive_ref[l]
        for c in range(ncomp):
            x = x_ref[l, c]
            x_up = jnp.where(first_row, up_ref[pl.ds(l * ncomp + c, 1), :], pltpu.roll(x, 1, 0))
            x_dn = jnp.where(last_row, down_ref[pl.ds(l * ncomp + c, 1), :], pltpu.roll(x, R - 1, 0))
            inplane = k_mid * (
                k_up * (x_up - x) + k_dn * (x_dn - x) + k_r * (shr(x) - x) + k_l * (shl(x) - x)
            )
            if l == 0:
                prev_src, prev_row = prevf_ref[pl.ds(c * R, R), :], below_ref[pl.ds(c, 1), :]
            else:
                prev_src, prev_row = x_ref[l - 1, c], down_ref[pl.ds((l - 1) * ncomp + c, 1), :]
            if l == L - 1:
                next_src, next_row = nextf_ref[pl.ds(c * R, R), :], below_ref[pl.ds(ncomp + c, 1), :]
            else:
                next_src, next_row = x_ref[l + 1, c], down_ref[pl.ds((l + 1) * ncomp + c, 1), :]
            part_row = below_ref[pl.ds((2 + l) * ncomp + c, 1), :]
            pull = scal_ref[l, 0] * (warp_of(prev_src, prev_row, ws[0]) - x)
            pull = pull + scal_ref[l, 1] * (warp_of(next_src, next_row, ws[1]) - x)
            pull = pull + scal_ref[l, 2] * (warp_of(part_ref[l, pl.ds(c * R, R), :], part_row, ws[2]) - x)
            force = inplane + pull
            vel = alive * (DAMPING * v_ref[l, c] + STEP * force)
            vo_ref[l, c] = vel
            new = x + STEP * vel
            xo_ref[l, c] = new
            if l == L - 1:
                lastf_ref[pl.ds(c * R, R), :] = new
            if l == 0:
                firstf_ref[pl.ds(c * R, R), :] = new
            top_ref[pl.ds(l * ncomp + c, 1), :] = new[0:1]
            bot_ref[pl.ds(l * ncomp + c, 1), :] = new[R - 1 : R]
    for d in range(send_ref.shape[0]):
        for c in range(ncomp):
            send_ref[d, pl.ds(c * R, R), :] = xo_ref[sel_ref[d], c]


def update(scal, sel, x, v, kst, alive, part, up, down, prevf, nextf, below):
    nb = sel.shape[0]
    vmem = pl.BlockSpec(memory_space=pltpu.VMEM)
    smem = pl.BlockSpec(memory_space=pltpu.SMEM)
    moved = 4 * (3 * x.size + kst.size + alive.size + part.size + 3 * x[0].size + nb * x[0].size)
    return pl.pallas_call(
        update_kernel,
        out_shape=(
            jax.ShapeDtypeStruct(x.shape, x.dtype),
            jax.ShapeDtypeStruct(x.shape, x.dtype),
            jax.ShapeDtypeStruct((nb, x.shape[1] * x.shape[2], x.shape[3]), x.dtype),
            jax.ShapeDtypeStruct((x.shape[1] * x.shape[2], x.shape[3]), x.dtype),
            jax.ShapeDtypeStruct((x.shape[1] * x.shape[2], x.shape[3]), x.dtype),
            jax.ShapeDtypeStruct((x.shape[0] * x.shape[1], x.shape[3]), x.dtype),
            jax.ShapeDtypeStruct((x.shape[0] * x.shape[1], x.shape[3]), x.dtype),
        ),
        in_specs=[smem, smem] + [vmem] * 10,
        out_specs=[vmem] * 7,
        compiler_params=pltpu.CompilerParams(vmem_limit_bytes=48 * 1024 * 1024),
        cost_estimate=pl.CostEstimate(flops=80 * x.size, bytes_accessed=moved, transcendentals=0),
    )(scal, sel, x, v, kst, alive, part, up, down, prevf, nextf, below)


def body(disp, vel, stiff_class, valid, class_table, warp, spring_z, skip_partner):
    local_count = disp.shape[0]
    block_count = lax.axis_size("gz")
    block_index = lax.axis_index("gz")
    total = local_count * block_count
    alive = valid.astype(jnp.float32)
    kappa = jnp.zeros(stiff_class.shape, jnp.float32)
    for level in range(class_table.shape[0]):
        kappa = jnp.where(stiff_class == level, class_table[level], kappa)
    kappa = kappa * alive
    stiff = jnp.stack([kappa, alive])
    stiff_ext = jnp.concatenate(
        [
            shift_rows(stiff[:, :, -1:], "tile", True),
            stiff,
            shift_rows(stiff[:, :, :1], "tile", False),
        ],
        axis=2,
    )
    kap_ext = stiff_ext[0]
    alive_mid = alive
    global_ids = block_index * local_count + jnp.arange(local_count, dtype=jnp.int32)
    has_prev = (global_ids > 0).astype(jnp.float32)
    has_next = (global_ids < total - 1).astype(jnp.float32)

    mine = lax.dynamic_slice_in_dim(skip_partner, block_index * local_count, local_count, 0)
    src_block = mine // local_count
    wanted = skip_partner.reshape(block_count, local_count)
    hit = (wanted // local_count) == block_index
    send_sel = jnp.sum(jnp.where(hit, wanted % local_count, 0), axis=1)

    k_mid = kap_ext[:, 1:-1]
    kst = jnp.stack([kap_ext[:, :-2], k_mid, kap_ext[:, 2:], shift_right(k_mid), shift_left(k_mid)])
    scal = jnp.concatenate(
        [
            (spring_z[:, 0] * has_prev)[:, None],
            (spring_z[:, 1] * has_next)[:, None],
            spring_z[:, 2:3],
            warp.reshape(local_count, 6),
        ],
        axis=1,
    )
    ncomp = disp.shape[1]
    cols = disp.shape[3]

    field = disp
    velocity = vel
    send = field[0][None]
    for l in range(1, local_count):
        send = jnp.where((send_sel == l)[:, None, None, None], field[l][None], send)
    plane = ncomp * disp.shape[2]
    send = send.reshape(block_count, plane, cols)
    last_face = field[-1].reshape(plane, cols)
    first_face = field[0].reshape(plane, cols)
    top_rows = field[:, :, 0].reshape(local_count * ncomp, cols)
    bot_rows = field[:, :, -1].reshape(local_count * ncomp, cols)
    for _ in range(ITERS):
      recv = lax.all_to_all(send, "gz", 0, 0, tiled=True)
      partner8 = jnp.stack(
          [lax.dynamic_index_in_dim(recv, src_block[l], 0, keepdims=False) for l in range(local_count)]
      )
      prev_face = shift_rows(last_face, "gz", True)
      next_face = shift_rows(first_face, "gz", False)
      up = shift_rows(bot_rows, "tile", True)
      down = shift_rows(top_rows, "tile", False)
      rows = disp.shape[2]
      heads = [prev_face[c * rows : c * rows + 1] for c in range(ncomp)]
      heads += [next_face[c * rows : c * rows + 1] for c in range(ncomp)]
      heads += [
          lax.dynamic_slice(recv, (src_block[l], c * rows, 0), (1, 1, cols))[0]
          for l in range(local_count)
          for c in range(ncomp)
      ]
      firsts = jnp.concatenate(heads, axis=0)
      below = shift_rows(firsts, "tile", False)
      field, velocity, send, last_face, first_face, top_rows, bot_rows = update(
          scal,
          send_sel,
          field,
          velocity,
          kst,
          alive_mid,
          partner8,
          up,
          down,
          prev_face,
          next_face,
          below,
      )
    return (field, velocity)


def solution(mesh):
    placed = (
        P("gz", None, "tile", None),
        P("gz", None, "tile", None),
        P("gz", "tile", None),
        P("gz", "tile", None),
        P(),
        P("gz", None, None),
        P("gz", None),
        P(),
    )
    return jax.shard_map(
        body,
        mesh=mesh,
        in_specs=placed,
        out_specs=(P("gz", None, "tile", None), P("gz", None, "tile", None)),
        check_vma=False,
    )
```

```python
import jax
import jax.numpy as jnp
from jax import lax
from jax.experimental import pallas as pl
from jax.experimental.pallas import tpu as pltpu
from jax.sharding import PartitionSpec as P


ITERS = 3


DAMPING = 0.9
STEP = 0.1


def shift_rows(block, axis, forward):
    count = lax.axis_size(axis)
    pairs = [(i, i + 1) for i in range(count - 1)]
    if not forward:
        pairs = [(t, s) for s, t in pairs]
    return lax.ppermute(block, axis, pairs)


def shift_left(field):
    return jnp.concatenate([field[..., 1:], jnp.zeros_like(field[..., :1])], axis=-1)


def shift_right(field):
    return jnp.concatenate([jnp.zeros_like(field[..., :1]), field[..., :-1]], axis=-1)


def update_kernel(scal_ref, sel_ref, x_ref, v_ref, k_ref, alive_ref, part_ref, up_ref, down_ref,
                  prevf_ref, nextf_ref, below_ref, xo_ref, vo_ref, send_ref, lastf_ref, firstf_ref,
                  top_ref, bot_ref):
    L, ncomp, R, C = x_ref.shape
    rows = lax.broadcasted_iota(jnp.int32, (R, C), 0)
    cols = lax.broadcasted_iota(jnp.int32, (R, C), 1)
    first_row = rows == 0
    last_row = rows == R - 1

    def shl(a):
        return jnp.where(cols == C - 1, 0.0, pltpu.roll(a, C - 1, 1))

    def shr(a):
        return jnp.where(cols == 0, 0.0, pltpu.roll(a, 1, 1))

    def warp_of(src, row8, w):
        lower = jnp.where(last_row, row8, pltpu.roll(src, R - 1, 0))
        return w[0] * src + w[1] * shl(src) + w[2] * lower + w[3] * shl(lower)

    for l in range(L):
        ws = []
        for k in range(3):
            a = scal_ref[l, 3 + 2 * k]
            b = scal_ref[l, 4 + 2 * k]
            ws.append(((1.0 - a) * (1.0 - b), (1.0 - a) * b, a * (1.0 - b), a * b))
        k_up = k_ref[0, l]
        k_mid = k_ref[1, l]
        k_dn = k_ref[2, l]
        k_r = k_ref[3, l]
        k_l = k_ref[4, l]
        alive = alive_ref[l]
        for c in range(ncomp):
            x = x_ref[l, c]
            x_up = jnp.where(first_row, up_ref[pl.ds(l * ncomp + c, 1), :], pltpu.roll(x, 1, 0))
            x_dn = jnp.where(last_row, down_ref[pl.ds(l * ncomp + c, 1), :], pltpu.roll(x, R - 1, 0))
            inplane = k_mid * (
                k_up * (x_up - x) + k_dn * (x_dn - x) + k_r * (shr(x) - x) + k_l * (shl(x) - x)
            )
            if l == 0:
                prev_src, prev_row = prevf_ref[pl.ds(c * R, R), :], below_ref[pl.ds(c, 1), :]
            else:
                prev_src, prev_row = x_ref[l - 1, c], down_ref[pl.ds((l - 1) * ncomp + c, 1), :]
            if l == L - 1:
                next_src, next_row = nextf_ref[pl.ds(c * R, R), :], below_ref[pl.ds(ncomp + c, 1), :]
            else:
                next_src, next_row = x_ref[l + 1, c], down_ref[pl.ds((l + 1) * ncomp + c, 1), :]
            part_row = below_ref[pl.ds((2 + l) * ncomp + c, 1), :]
            pull = scal_ref[l, 0] * (warp_of(prev_src, prev_row, ws[0]) - x)
            pull = pull + scal_ref[l, 1] * (warp_of(next_src, next_row, ws[1]) - x)
            pull = pull + scal_ref[l, 2] * (warp_of(part_ref[l, pl.ds(c * R, R), :], part_row, ws[2]) - x)
            force = inplane + pull
            vel = alive * (DAMPING * v_ref[l, c] + STEP * force)
            vo_ref[l, c] = vel
            new = x + STEP * vel
            xo_ref[l, c] = new
            if l == L - 1:
                lastf_ref[pl.ds(c * R, R), :] = new
            if l == 0:
                firstf_ref[pl.ds(c * R, R), :] = new
            top_ref[pl.ds(l * ncomp + c, 1), :] = new[0:1]
            bot_ref[pl.ds(l * ncomp + c, 1), :] = new[R - 1 : R]
    for d in range(send_ref.shape[0]):
        for c in range(ncomp):
            send_ref[d, pl.ds(c * R, R), :] = xo_ref[sel_ref[d], c]


def update(scal, sel, x, v, kst, alive, part, up, down, prevf, nextf, below):
    nb = sel.shape[0]
    vmem = pl.BlockSpec(memory_space=pltpu.VMEM)
    smem = pl.BlockSpec(memory_space=pltpu.SMEM)
    moved = 4 * (3 * x.size + kst.size + alive.size + part.size + 3 * x[0].size + nb * x[0].size)
    return pl.pallas_call(
        update_kernel,
        out_shape=(
            jax.ShapeDtypeStruct(x.shape, x.dtype),
            jax.ShapeDtypeStruct(x.shape, x.dtype),
            jax.ShapeDtypeStruct((nb, x.shape[1] * x.shape[2], x.shape[3]), x.dtype),
            jax.ShapeDtypeStruct((x.shape[1] * x.shape[2], x.shape[3]), x.dtype),
            jax.ShapeDtypeStruct((x.shape[1] * x.shape[2], x.shape[3]), x.dtype),
            jax.ShapeDtypeStruct((x.shape[0] * x.shape[1], x.shape[3]), x.dtype),
            jax.ShapeDtypeStruct((x.shape[0] * x.shape[1], x.shape[3]), x.dtype),
        ),
        in_specs=[smem, smem] + [vmem] * 10,
        out_specs=[vmem] * 7,
        compiler_params=pltpu.CompilerParams(vmem_limit_bytes=48 * 1024 * 1024),
        cost_estimate=pl.CostEstimate(flops=80 * x.size, bytes_accessed=moved, transcendentals=0),
    )(scal, sel, x, v, kst, alive, part, up, down, prevf, nextf, below)


def body(disp, vel, stiff_class, valid, class_table, warp, spring_z, skip_partner):
    local_count = disp.shape[0]
    block_count = lax.axis_size("gz")
    block_index = lax.axis_index("gz")
    total = local_count * block_count
    alive = valid.astype(jnp.float32)
    kappa = jnp.zeros(stiff_class.shape, jnp.float32)
    for level in range(class_table.shape[0]):
        kappa = jnp.where(stiff_class == level, class_table[level], kappa)
    kappa = kappa * alive
    stiff = jnp.stack([kappa, alive])
    stiff_ext = jnp.concatenate(
        [
            shift_rows(stiff[:, :, -1:], "tile", True),
            stiff,
            shift_rows(stiff[:, :, :1], "tile", False),
        ],
        axis=2,
    )
    kap_ext = stiff_ext[0]
    alive_mid = alive
    global_ids = block_index * local_count + jnp.arange(local_count, dtype=jnp.int32)
    has_prev = (global_ids > 0).astype(jnp.float32)
    has_next = (global_ids < total - 1).astype(jnp.float32)

    mine = lax.dynamic_slice_in_dim(skip_partner, block_index * local_count, local_count, 0)
    src_block = mine // local_count
    wanted = skip_partner.reshape(block_count, local_count)
    hit = (wanted // local_count) == block_index
    send_sel = jnp.sum(jnp.where(hit, wanted % local_count, 0), axis=1)

    k_mid = kap_ext[:, 1:-1]
    kst = jnp.stack([kap_ext[:, :-2], k_mid, kap_ext[:, 2:], shift_right(k_mid), shift_left(k_mid)])
    scal = jnp.concatenate(
        [
            (spring_z[:, 0] * has_prev)[:, None],
            (spring_z[:, 1] * has_next)[:, None],
            spring_z[:, 2:3],
            warp.reshape(local_count, 6),
        ],
        axis=1,
    )
    ncomp = disp.shape[1]
    cols = disp.shape[3]

    field = disp
    velocity = vel
    plane = ncomp * disp.shape[2]
    send = jnp.take(field.reshape(local_count, plane, cols), send_sel, axis=0, mode="clip")
    last_face = field[-1].reshape(plane, cols)
    first_face = field[0].reshape(plane, cols)
    top_rows = field[:, :, 0].reshape(local_count * ncomp, cols)
    bot_rows = field[:, :, -1].reshape(local_count * ncomp, cols)
    for _ in range(ITERS):
      recv = lax.all_to_all(send, "gz", 0, 0, tiled=True)
      partner8 = jnp.stack(
          [lax.dynamic_index_in_dim(recv, src_block[l], 0, keepdims=False) for l in range(local_count)]
      )
      prev_face = shift_rows(last_face, "gz", True)
      next_face = shift_rows(first_face, "gz", False)
      up = shift_rows(bot_rows, "tile", True)
      down = shift_rows(top_rows, "tile", False)
      rows = disp.shape[2]
      heads = [prev_face[c * rows : c * rows + 1] for c in range(ncomp)]
      heads += [next_face[c * rows : c * rows + 1] for c in range(ncomp)]
      heads += [
          lax.dynamic_slice(recv, (src_block[l], c * rows, 0), (1, 1, cols))[0]
          for l in range(local_count)
          for c in range(ncomp)
      ]
      firsts = jnp.concatenate(heads, axis=0)
      below = shift_rows(firsts, "tile", False)
      field, velocity, send, last_face, first_face, top_rows, bot_rows = update(
          scal,
          send_sel,
          field,
          velocity,
          kst,
          alive_mid,
          partner8,
          up,
          down,
          prev_face,
          next_face,
          below,
      )
    return (field, velocity)


def solution(mesh):
    placed = (
        P("gz", None, "tile", None),
        P("gz", None, "tile", None),
        P("gz", "tile", None),
        P("gz", "tile", None),
        P(),
        P("gz", None, None),
        P("gz", None),
        P(),
    )
    return jax.shard_map(
        body,
        mesh=mesh,
        in_specs=placed,
        out_specs=(P("gz", None, "tile", None), P("gz", None, "tile", None)),
        check_vma=False,
    )
```

```python
import jax
import jax.numpy as jnp
from jax import lax
from jax.experimental import pallas as pl
from jax.experimental.pallas import tpu as pltpu
from jax.sharding import PartitionSpec as P


ITERS = 3


DAMPING = 0.9
STEP = 0.1


def shift_rows(block, axis, forward):
    count = lax.axis_size(axis)
    pairs = [(i, i + 1) for i in range(count - 1)]
    if not forward:
        pairs = [(t, s) for s, t in pairs]
    return lax.ppermute(block, axis, pairs)


def shift_left(field):
    return jnp.concatenate([field[..., 1:], jnp.zeros_like(field[..., :1])], axis=-1)


def shift_right(field):
    return jnp.concatenate([jnp.zeros_like(field[..., :1]), field[..., :-1]], axis=-1)


def update_kernel(scal_ref, sel_ref, x_ref, v_ref, k_ref, alive_ref, part_ref, up_ref, down_ref,
                  prevf_ref, nextf_ref, below_ref, xo_ref, vo_ref, send_ref, lastf_ref, firstf_ref,
                  top_ref, bot_ref):
    L, ncomp, R, C = x_ref.shape
    rows = lax.broadcasted_iota(jnp.int32, (R, C), 0)
    cols = lax.broadcasted_iota(jnp.int32, (R, C), 1)
    first_row = rows == 0
    last_row = rows == R - 1

    def shl(a):
        return jnp.where(cols == C - 1, 0.0, pltpu.roll(a, C - 1, 1))

    def shr(a):
        return jnp.where(cols == 0, 0.0, pltpu.roll(a, 1, 1))

    def warp_of(src, row8, w):
        lower = jnp.where(last_row, row8, pltpu.roll(src, R - 1, 0))
        return w[0] * src + w[1] * shl(src) + w[2] * lower + w[3] * shl(lower)

    for l in range(L):
        ws = []
        for k in range(3):
            a = scal_ref[l, 3 + 2 * k]
            b = scal_ref[l, 4 + 2 * k]
            ws.append(((1.0 - a) * (1.0 - b), (1.0 - a) * b, a * (1.0 - b), a * b))
        k_up = k_ref[0, l]
        k_mid = k_ref[1, l]
        k_dn = k_ref[2, l]
        k_r = k_ref[3, l]
        k_l = k_ref[4, l]
        alive = alive_ref[l]
        for c in range(ncomp):
            x = x_ref[l, c]
            x_up = jnp.where(first_row, up_ref[pl.ds(l * ncomp + c, 1), :], pltpu.roll(x, 1, 0))
            x_dn = jnp.where(last_row, down_ref[pl.ds(l * ncomp + c, 1), :], pltpu.roll(x, R - 1, 0))
            inplane = k_mid * (
                k_up * (x_up - x) + k_dn * (x_dn - x) + k_r * (shr(x) - x) + k_l * (shl(x) - x)
            )
            if l == 0:
                prev_src, prev_row = prevf_ref[pl.ds(c * R, R), :], below_ref[pl.ds(c, 1), :]
            else:
                prev_src, prev_row = x_ref[l - 1, c], down_ref[pl.ds((l - 1) * ncomp + c, 1), :]
            if l == L - 1:
                next_src, next_row = nextf_ref[pl.ds(c * R, R), :], below_ref[pl.ds(ncomp + c, 1), :]
            else:
                next_src, next_row = x_ref[l + 1, c], down_ref[pl.ds((l + 1) * ncomp + c, 1), :]
            part_row = below_ref[pl.ds((2 + l) * ncomp + c, 1), :]
            pull = scal_ref[l, 0] * (warp_of(prev_src, prev_row, ws[0]) - x)
            pull = pull + scal_ref[l, 1] * (warp_of(next_src, next_row, ws[1]) - x)
            pull = pull + scal_ref[l, 2] * (warp_of(part_ref[l, pl.ds(c * R, R), :], part_row, ws[2]) - x)
            force = inplane + pull
            vel = alive * (DAMPING * v_ref[l, c] + STEP * force)
            vo_ref[l, c] = vel
            new = x + STEP * vel
            xo_ref[l, c] = new
            if l == L - 1:
                lastf_ref[pl.ds(c * R, R), :] = new
            if l == 0:
                firstf_ref[pl.ds(c * R, R), :] = new
            top_ref[pl.ds(l * ncomp + c, 1), :] = new[0:1]
            bot_ref[pl.ds(l * ncomp + c, 1), :] = new[R - 1 : R]
    for d in range(send_ref.shape[0]):
        for c in range(ncomp):
            send_ref[d, pl.ds(c * R, R), :] = xo_ref[sel_ref[d], c]


def update(scal, sel, x, v, kst, alive, part, up, down, prevf, nextf, below):
    nb = sel.shape[0]
    vmem = pl.BlockSpec(memory_space=pltpu.VMEM)
    smem = pl.BlockSpec(memory_space=pltpu.SMEM)
    moved = 4 * (3 * x.size + kst.size + alive.size + part.size + 3 * x[0].size + nb * x[0].size)
    return pl.pallas_call(
        update_kernel,
        out_shape=(
            jax.ShapeDtypeStruct(x.shape, x.dtype),
            jax.ShapeDtypeStruct(x.shape, x.dtype),
            jax.ShapeDtypeStruct((nb, x.shape[1] * x.shape[2], x.shape[3]), x.dtype),
            jax.ShapeDtypeStruct((x.shape[1] * x.shape[2], x.shape[3]), x.dtype),
            jax.ShapeDtypeStruct((x.shape[1] * x.shape[2], x.shape[3]), x.dtype),
            jax.ShapeDtypeStruct((x.shape[0] * x.shape[1], x.shape[3]), x.dtype),
            jax.ShapeDtypeStruct((x.shape[0] * x.shape[1], x.shape[3]), x.dtype),
        ),
        in_specs=[smem, smem] + [vmem] * 10,
        out_specs=[vmem] * 7,
        compiler_params=pltpu.CompilerParams(vmem_limit_bytes=48 * 1024 * 1024),
        cost_estimate=pl.CostEstimate(flops=80 * x.size, bytes_accessed=moved, transcendentals=0),
    )(scal, sel, x, v, kst, alive, part, up, down, prevf, nextf, below)


def send_kernel(sel_ref, x_ref, send_ref):
    ncomp, R = x_ref.shape[1], x_ref.shape[2]
    for d in range(send_ref.shape[0]):
        for c in range(ncomp):
            send_ref[d, pl.ds(c * R, R), :] = x_ref[sel_ref[d], c]


def first_send(sel, x):
    nb = sel.shape[0]
    return pl.pallas_call(
        send_kernel,
        out_shape=jax.ShapeDtypeStruct((nb, x.shape[1] * x.shape[2], x.shape[3]), x.dtype),
        in_specs=[pl.BlockSpec(memory_space=pltpu.SMEM), pl.BlockSpec(memory_space=pltpu.VMEM)],
        out_specs=pl.BlockSpec(memory_space=pltpu.VMEM),
        cost_estimate=pl.CostEstimate(flops=0, bytes_accessed=4 * (x.size + nb * x[0].size), transcendentals=0),
    )(sel, x)


def body(disp, vel, stiff_class, valid, class_table, warp, spring_z, skip_partner):
    local_count = disp.shape[0]
    block_count = lax.axis_size("gz")
    block_index = lax.axis_index("gz")
    total = local_count * block_count
    alive = valid.astype(jnp.float32)
    kappa = jnp.zeros(stiff_class.shape, jnp.float32)
    for level in range(class_table.shape[0]):
        kappa = jnp.where(stiff_class == level, class_table[level], kappa)
    kappa = kappa * alive
    stiff = jnp.stack([kappa, alive])
    stiff_ext = jnp.concatenate(
        [
            shift_rows(stiff[:, :, -1:], "tile", True),
            stiff,
            shift_rows(stiff[:, :, :1], "tile", False),
        ],
        axis=2,
    )
    kap_ext = stiff_ext[0]
    alive_mid = alive
    global_ids = block_index * local_count + jnp.arange(local_count, dtype=jnp.int32)
    has_prev = (global_ids > 0).astype(jnp.float32)
    has_next = (global_ids < total - 1).astype(jnp.float32)

    mine = lax.dynamic_slice_in_dim(skip_partner, block_index * local_count, local_count, 0)
    src_block = mine // local_count
    wanted = skip_partner.reshape(block_count, local_count)
    hit = (wanted // local_count) == block_index
    send_sel = jnp.sum(jnp.where(hit, wanted % local_count, 0), axis=1)

    k_mid = kap_ext[:, 1:-1]
    kst = jnp.stack([kap_ext[:, :-2], k_mid, kap_ext[:, 2:], shift_right(k_mid), shift_left(k_mid)])
    scal = jnp.concatenate(
        [
            (spring_z[:, 0] * has_prev)[:, None],
            (spring_z[:, 1] * has_next)[:, None],
            spring_z[:, 2:3],
            warp.reshape(local_count, 6),
        ],
        axis=1,
    )
    ncomp = disp.shape[1]
    cols = disp.shape[3]

    field = disp
    velocity = vel
    plane = ncomp * disp.shape[2]
    send = first_send(send_sel, field)
    last_face = field[-1].reshape(plane, cols)
    first_face = field[0].reshape(plane, cols)
    top_rows = field[:, :, 0].reshape(local_count * ncomp, cols)
    bot_rows = field[:, :, -1].reshape(local_count * ncomp, cols)
    for _ in range(ITERS):
      recv = lax.all_to_all(send, "gz", 0, 0, tiled=True)
      partner8 = jnp.stack(
          [lax.dynamic_index_in_dim(recv, src_block[l], 0, keepdims=False) for l in range(local_count)]
      )
      prev_face = shift_rows(last_face, "gz", True)
      next_face = shift_rows(first_face, "gz", False)
      up = shift_rows(bot_rows, "tile", True)
      down = shift_rows(top_rows, "tile", False)
      rows = disp.shape[2]
      heads = [prev_face[c * rows : c * rows + 1] for c in range(ncomp)]
      heads += [next_face[c * rows : c * rows + 1] for c in range(ncomp)]
      heads += [
          lax.dynamic_slice(recv, (src_block[l], c * rows, 0), (1, 1, cols))[0]
          for l in range(local_count)
          for c in range(ncomp)
      ]
      firsts = jnp.concatenate(heads, axis=0)
      below = shift_rows(firsts, "tile", False)
      field, velocity, send, last_face, first_face, top_rows, bot_rows = update(
          scal,
          send_sel,
          field,
          velocity,
          kst,
          alive_mid,
          partner8,
          up,
          down,
          prev_face,
          next_face,
          below,
      )
    return (field, velocity)


def solution(mesh):
    placed = (
        P("gz", None, "tile", None),
        P("gz", None, "tile", None),
        P("gz", "tile", None),
        P("gz", "tile", None),
        P(),
        P("gz", None, None),
        P("gz", None),
        P(),
    )
    return jax.shard_map(
        body,
        mesh=mesh,
        in_specs=placed,
        out_specs=(P("gz", None, "tile", None), P("gz", None, "tile", None)),
        check_vma=False,
    )
```

```python
import jax
import jax.numpy as jnp
from jax import lax
from jax.experimental import pallas as pl
from jax.experimental.pallas import tpu as pltpu
from jax.sharding import PartitionSpec as P


ITERS = 3


DAMPING = 0.9
STEP = 0.1


def shift_rows(block, axis, forward):
    count = lax.axis_size(axis)
    pairs = [(i, i + 1) for i in range(count - 1)]
    if not forward:
        pairs = [(t, s) for s, t in pairs]
    return lax.ppermute(block, axis, pairs)


def shift_left(field):
    return jnp.concatenate([field[..., 1:], jnp.zeros_like(field[..., :1])], axis=-1)


def shift_right(field):
    return jnp.concatenate([jnp.zeros_like(field[..., :1]), field[..., :-1]], axis=-1)


def update_kernel(scal_ref, sel_ref, x_ref, v_ref, k_ref, alive_ref, part_ref, up_ref, down_ref,
                  prevf_ref, nextf_ref, below_ref, xo_ref, vo_ref, send_ref=None, lastf_ref=None,
                  firstf_ref=None, top_ref=None, bot_ref=None):
    tail = send_ref is None
    L, ncomp, R, C = x_ref.shape
    rows = lax.broadcasted_iota(jnp.int32, (R, C), 0)
    cols = lax.broadcasted_iota(jnp.int32, (R, C), 1)
    first_row = rows == 0
    last_row = rows == R - 1

    def shl(a):
        return jnp.where(cols == C - 1, 0.0, pltpu.roll(a, C - 1, 1))

    def shr(a):
        return jnp.where(cols == 0, 0.0, pltpu.roll(a, 1, 1))

    def warp_of(src, row8, w):
        lower = jnp.where(last_row, row8, pltpu.roll(src, R - 1, 0))
        return w[0] * src + w[1] * shl(src) + w[2] * lower + w[3] * shl(lower)

    for l in range(L):
        ws = []
        for k in range(3):
            a = scal_ref[l, 3 + 2 * k]
            b = scal_ref[l, 4 + 2 * k]
            ws.append(((1.0 - a) * (1.0 - b), (1.0 - a) * b, a * (1.0 - b), a * b))
        k_up = k_ref[0, l]
        k_mid = k_ref[1, l]
        k_dn = k_ref[2, l]
        k_r = k_ref[3, l]
        k_l = k_ref[4, l]
        alive = alive_ref[l]
        for c in range(ncomp):
            x = x_ref[l, c]
            x_up = jnp.where(first_row, up_ref[pl.ds(l * ncomp + c, 1), :], pltpu.roll(x, 1, 0))
            x_dn = jnp.where(last_row, down_ref[pl.ds(l * ncomp + c, 1), :], pltpu.roll(x, R - 1, 0))
            inplane = k_mid * (
                k_up * (x_up - x) + k_dn * (x_dn - x) + k_r * (shr(x) - x) + k_l * (shl(x) - x)
            )
            if l == 0:
                prev_src, prev_row = prevf_ref[pl.ds(c * R, R), :], below_ref[pl.ds(c, 1), :]
            else:
                prev_src, prev_row = x_ref[l - 1, c], down_ref[pl.ds((l - 1) * ncomp + c, 1), :]
            if l == L - 1:
                next_src, next_row = nextf_ref[pl.ds(c * R, R), :], below_ref[pl.ds(ncomp + c, 1), :]
            else:
                next_src, next_row = x_ref[l + 1, c], down_ref[pl.ds((l + 1) * ncomp + c, 1), :]
            part_row = below_ref[pl.ds((2 + l) * ncomp + c, 1), :]
            pull = scal_ref[l, 0] * (warp_of(prev_src, prev_row, ws[0]) - x)
            pull = pull + scal_ref[l, 1] * (warp_of(next_src, next_row, ws[1]) - x)
            pull = pull + scal_ref[l, 2] * (warp_of(part_ref[l, pl.ds(c * R, R), :], part_row, ws[2]) - x)
            force = inplane + pull
            vel = alive * (DAMPING * v_ref[l, c] + STEP * force)
            vo_ref[l, c] = vel
            new = x + STEP * vel
            xo_ref[l, c] = new
            if tail:
                continue
            if l == L - 1:
                lastf_ref[pl.ds(c * R, R), :] = new
            if l == 0:
                firstf_ref[pl.ds(c * R, R), :] = new
            top_ref[pl.ds(l * ncomp + c, 1), :] = new[0:1]
            bot_ref[pl.ds(l * ncomp + c, 1), :] = new[R - 1 : R]
    if tail:
        return
    for d in range(send_ref.shape[0]):
        for c in range(ncomp):
            send_ref[d, pl.ds(c * R, R), :] = xo_ref[sel_ref[d], c]


def update(tail, scal, sel, x, v, kst, alive, part, up, down, prevf, nextf, below):
    nb = sel.shape[0]
    vmem = pl.BlockSpec(memory_space=pltpu.VMEM)
    smem = pl.BlockSpec(memory_space=pltpu.SMEM)
    moved = 4 * (3 * x.size + kst.size + alive.size + part.size + 3 * x[0].size + nb * x[0].size)
    return pl.pallas_call(
        update_kernel,
        out_shape=(
            jax.ShapeDtypeStruct(x.shape, x.dtype),
            jax.ShapeDtypeStruct(x.shape, x.dtype),
        )
        if tail
        else (
            jax.ShapeDtypeStruct(x.shape, x.dtype),
            jax.ShapeDtypeStruct(x.shape, x.dtype),
            jax.ShapeDtypeStruct((nb, x.shape[1] * x.shape[2], x.shape[3]), x.dtype),
            jax.ShapeDtypeStruct((x.shape[1] * x.shape[2], x.shape[3]), x.dtype),
            jax.ShapeDtypeStruct((x.shape[1] * x.shape[2], x.shape[3]), x.dtype),
            jax.ShapeDtypeStruct((x.shape[0] * x.shape[1], x.shape[3]), x.dtype),
            jax.ShapeDtypeStruct((x.shape[0] * x.shape[1], x.shape[3]), x.dtype),
        ),
        in_specs=[smem, smem] + [vmem] * 10,
        out_specs=[vmem] * (2 if tail else 7),
        compiler_params=pltpu.CompilerParams(vmem_limit_bytes=48 * 1024 * 1024),
        cost_estimate=pl.CostEstimate(flops=80 * x.size, bytes_accessed=moved, transcendentals=0),
    )(scal, sel, x, v, kst, alive, part, up, down, prevf, nextf, below)


def send_kernel(sel_ref, x_ref, send_ref):
    ncomp, R = x_ref.shape[1], x_ref.shape[2]
    for d in range(send_ref.shape[0]):
        for c in range(ncomp):
            send_ref[d, pl.ds(c * R, R), :] = x_ref[sel_ref[d], c]


def first_send(sel, x):
    nb = sel.shape[0]
    return pl.pallas_call(
        send_kernel,
        out_shape=jax.ShapeDtypeStruct((nb, x.shape[1] * x.shape[2], x.shape[3]), x.dtype),
        in_specs=[pl.BlockSpec(memory_space=pltpu.SMEM), pl.BlockSpec(memory_space=pltpu.VMEM)],
        out_specs=pl.BlockSpec(memory_space=pltpu.VMEM),
        cost_estimate=pl.CostEstimate(flops=0, bytes_accessed=4 * (x.size + nb * x[0].size), transcendentals=0),
    )(sel, x)


def body(disp, vel, stiff_class, valid, class_table, warp, spring_z, skip_partner):
    local_count = disp.shape[0]
    block_count = lax.axis_size("gz")
    block_index = lax.axis_index("gz")
    total = local_count * block_count
    alive = valid.astype(jnp.float32)
    kappa = jnp.zeros(stiff_class.shape, jnp.float32)
    for level in range(class_table.shape[0]):
        kappa = jnp.where(stiff_class == level, class_table[level], kappa)
    kappa = kappa * alive
    stiff = jnp.stack([kappa, alive])
    stiff_ext = jnp.concatenate(
        [
            shift_rows(stiff[:, :, -1:], "tile", True),
            stiff,
            shift_rows(stiff[:, :, :1], "tile", False),
        ],
        axis=2,
    )
    kap_ext = stiff_ext[0]
    alive_mid = alive
    global_ids = block_index * local_count + jnp.arange(local_count, dtype=jnp.int32)
    has_prev = (global_ids > 0).astype(jnp.float32)
    has_next = (global_ids < total - 1).astype(jnp.float32)

    mine = lax.dynamic_slice_in_dim(skip_partner, block_index * local_count, local_count, 0)
    src_block = mine // local_count
    wanted = skip_partner.reshape(block_count, local_count)
    hit = (wanted // local_count) == block_index
    send_sel = jnp.sum(jnp.where(hit, wanted % local_count, 0), axis=1)

    k_mid = kap_ext[:, 1:-1]
    kst = jnp.stack([kap_ext[:, :-2], k_mid, kap_ext[:, 2:], shift_right(k_mid), shift_left(k_mid)])
    scal = jnp.concatenate(
        [
            (spring_z[:, 0] * has_prev)[:, None],
            (spring_z[:, 1] * has_next)[:, None],
            spring_z[:, 2:3],
            warp.reshape(local_count, 6),
        ],
        axis=1,
    )
    ncomp = disp.shape[1]
    cols = disp.shape[3]

    field = disp
    velocity = vel
    plane = ncomp * disp.shape[2]
    send = first_send(send_sel, field)
    last_face = field[-1].reshape(plane, cols)
    first_face = field[0].reshape(plane, cols)
    top_rows = field[:, :, 0].reshape(local_count * ncomp, cols)
    bot_rows = field[:, :, -1].reshape(local_count * ncomp, cols)
    for step in range(ITERS):
      recv = lax.all_to_all(send, "gz", 0, 0, tiled=True)
      partner8 = jnp.stack(
          [lax.dynamic_index_in_dim(recv, src_block[l], 0, keepdims=False) for l in range(local_count)]
      )
      prev_face = shift_rows(last_face, "gz", True)
      next_face = shift_rows(first_face, "gz", False)
      up = shift_rows(bot_rows, "tile", True)
      down = shift_rows(top_rows, "tile", False)
      rows = disp.shape[2]
      heads = [prev_face[c * rows : c * rows + 1] for c in range(ncomp)]
      heads += [next_face[c * rows : c * rows + 1] for c in range(ncomp)]
      heads += [
          lax.dynamic_slice(recv, (src_block[l], c * rows, 0), (1, 1, cols))[0]
          for l in range(local_count)
          for c in range(ncomp)
      ]
      firsts = jnp.concatenate(heads, axis=0)
      below = shift_rows(firsts, "tile", False)
      outs = update(
          step == ITERS - 1,
          scal,
          send_sel,
          field,
          velocity,
          kst,
          alive_mid,
          partner8,
          up,
          down,
          prev_face,
          next_face,
          below,
      )
      if step == ITERS - 1:
          field, velocity = outs
      else:
          field, velocity, send, last_face, first_face, top_rows, bot_rows = outs
    return (field, velocity)


def solution(mesh):
    placed = (
        P("gz", None, "tile", None),
        P("gz", None, "tile", None),
        P("gz", "tile", None),
        P("gz", "tile", None),
        P(),
        P("gz", None, None),
        P("gz", None),
        P(),
    )
    return jax.shard_map(
        body,
        mesh=mesh,
        in_specs=placed,
        out_specs=(P("gz", None, "tile", None), P("gz", None, "tile", None)),
        check_vma=False,
    )
```
